512 devices in a mesh: lvl: 16 (over z), col: 32 (over y, x, core).
Axes of the slice: x: 4, y: 4, z: 16, core: 2. Of those that a mesh axis runs over, the one named last changes fastest.
Arguments:
- rhs: float32 [16, 1536, 128], P('lvl', 'col'), may hold values from -6 to 6
- panel: bfloat16 [16, 4, 1536, 1536], P('lvl', None, 'col'), may hold values from -0.078125 to 0.078125
- inverse_t: bfloat16 [16, 1536, 1536], P('lvl', 'col'), as said below
- pattern: int32 [16, 4, 12, 12], P('lvl'), may hold values 0 or 1
Outputs:
- sample: float32 [16, 1536, 128], P('lvl', 'col')
- solution: float32 [16, 1536, 128], P('lvl', 'col')
The draws below stay inside these ranges and needn't reach their ends.
Inputs may be any that keep to these rules, and one draw needn't show every extreme that they name: `pattern`: 1 marks a 128 x 128 tile of a panel slot that is structurally nonzero. Each inverse_t[s] is upper triangular with a positive diagonal.
All inputs are finite; a program needn't handle non-finite values.
Results may differ from the reference program's by a relative error of at most 0.035.
Values may be sent and summed in bfloat16 or wider, within the bound.
A program may use at most 64 MiB of HBM per device.

```python
import jax
import jax.numpy as jnp
from jax import lax

NB = 1536
BLOCK = 128
NRHS = 128
NSUP = 16
ANC = 4
KB = 12
ROWS = 48
N_COL = 32


def draw_inverse_t(key, part):
    off_key, diag_key = jax.random.split(jax.random.fold_in(key, 11))
    full_shape = (NSUP, NB, NB)
    row_ids = lax.broadcasted_iota(jnp.int32, full_shape, 1)
    col_ids = lax.broadcasted_iota(jnp.int32, full_shape, 2)
    spread = jax.random.normal(off_key, full_shape, jnp.float32) * 0.6 * (1.0 / NB) ** 0.5
    diagonal = jax.random.uniform(diag_key, (NSUP, NB, 1), jnp.float32, 0.8, 1.4)
    triangle = jnp.where(col_ids > row_ids, spread, 0.0) + jnp.where(col_ids == row_ids, diagonal, 0.0)
    return triangle.astype(jnp.bfloat16)


def place_ends(result, own_key, smallest, largest):
    longest = result.shape.index(max(result.shape))
    spots = []
    for shift in (0, 1):
        where = [jax.random.randint(jax.random.fold_in(own_key, axis), (), 0, length) for axis, length in enumerate(result.shape)]
        where[longest] = (where[longest] + shift) % result.shape[longest]
        spots.append(tuple(where))
    return result.at[spots[0]].set(smallest).at[spots[1]].set(largest)


def block_scale(own_key, dims, shards, least, high):
    factor_of, own = 1.0, jax.random.fold_in(own_key, 6)
    for dim, shards_of in shards:
        steps = jnp.exp(jax.random.uniform(jax.random.fold_in(own, dim), (shards_of,), jnp.float32, least / len(shards), high / len(shards)))
        factor_of = factor_of * jnp.repeat(steps, dims[dim] // shards_of).reshape([-1 if axis == dim else 1 for axis in range(len(dims))])
    return factor_of


def bell_draw(key, dims, width, reach, pieces=(), dtype=jnp.bfloat16):
    array = width * jax.random.normal(key, dims, jnp.float32)
    if pieces:
        array = array * block_scale(key, dims, pieces, -0.22, 0.18)
    return jnp.clip(array, -reach, reach).astype(dtype)


def setup_inputs(seed: int = 0) -> dict:
    key_list = jax.random.split(jax.random.key(seed), 5)
    rhs = bell_draw(key_list[0], (NSUP, NB, NRHS), 1.0, 6.0, ((0, 16), (1, 32)), jnp.float32)
    panel = bell_draw(key_list[1], (NSUP, ANC, NB, NB), (4 * NB) ** -0.5, 0.078125, ((0, 16), (2, 32)))
    inverse_t = draw_inverse_t(jax.random.fold_in(key_list[4], 71), 0)
    pattern = place_ends((jax.random.randint(key_list[3], (NSUP, ANC, KB, KB), 0, 4) < 3).astype(jnp.int32), jax.random.fold_in(key_list[3], 1), 0, 1)
    return {"rhs": rhs, "panel": panel, "inverse_t": inverse_t, "pattern": pattern}


def trailing_ones(position):
    ones_count = 0
    while position % 2 == 1:
        ones_count += 1
        position = position // 2
    return ones_count


def ancestor_list(node_id, node_total):
    chain_list = []
    while node_id != node_total - 1:
        depth_now = trailing_ones(node_id)
        step_size = 2 ** depth_now
        if (node_id // (2 * step_size)) % 2 == 0:
            node_id = node_id + step_size
        else:
            node_id = node_id - step_size
        chain_list.append(node_id)
    return chain_list


def rounded(quantity):
    return lax.optimization_barrier(quantity.astype(jnp.bfloat16)).astype(jnp.float32)


def reference(rhs, panel, inverse_t, pattern):
    levels = NSUP.bit_length() - 1
    chains = [ancestor_list(node_id, NSUP) for node_id in range(NSUP)]

    def slot_block(node_id, slot_pos):
        grown_mask = jnp.repeat(jnp.repeat(pattern[node_id, slot_pos], BLOCK, axis=0), BLOCK, axis=1)
        return panel[node_id, slot_pos] * grown_mask.astype(jnp.bfloat16)

    incoming = [jnp.zeros((NB, NRHS), jnp.float32) for node_id in range(NSUP)]
    sample = [None] * NSUP
    for section_num in range(levels + 1):
        for node_id in range(NSUP):
            if trailing_ones(node_id) != section_num:
                continue
            residual = (rhs[node_id] - incoming[node_id]).astype(jnp.bfloat16)
            inv_parts = inverse_t[node_id].reshape(N_COL, ROWS, NB).astype(jnp.float32)
            res_parts = residual.reshape(N_COL, ROWS, NRHS).astype(jnp.float32)
            part_sums = jnp.einsum('cri,crn->cin', inv_parts, res_parts)
            solved = jnp.sum(rounded(part_sums), axis=0)
            sample[node_id] = solved
            solved_half = solved.astype(jnp.bfloat16)
            for slot_pos, upper_id in enumerate(chains[node_id]):
                incoming[upper_id] = incoming[upper_id] + jnp.dot(slot_block(node_id, slot_pos), solved_half, preferred_element_type=jnp.float32)

    solution = [None] * NSUP
    solution_half = [None] * NSUP
    for section_num in range(levels, -1, -1):
        for node_id in range(NSUP):
            if trailing_ones(node_id) != section_num:
                continue
            chain_list = chains[node_id]
            if len(chain_list) > 0:
                depth_now = len(chain_list)
                blocks = jnp.stack([slot_block(node_id, slot_pos) for slot_pos in range(depth_now)]).astype(jnp.float32)
                ancestry = jnp.stack([solution_half[upper_id] for upper_id in chain_list]).astype(jnp.float32)
                part_sums = jnp.einsum('kcrn,kcrm->cnm', blocks.reshape(depth_now, N_COL, ROWS, NB), ancestry.reshape(depth_now, N_COL, ROWS, NRHS))
                adjoint = jnp.sum(rounded(part_sums), axis=0)
                back_full = sample[node_id] - adjoint
            else:
                back_full = sample[node_id]
            solved = jnp.dot(inverse_t[node_id], back_full.astype(jnp.bfloat16), preferred_element_type=jnp.float32)
            solution[node_id] = solved
            solution_half[node_id] = solved.astype(jnp.bfloat16)
    return jnp.stack(sample), jnp.stack(solution)
```

```python
import functools

import jax
import jax.numpy as jnp
from jax import lax
from jax.experimental import pallas as pl
from jax.experimental.pallas import tpu as pltpu
from jax.sharding import PartitionSpec as P

MESH = pl.DeviceIdType.MESH
NT = (((1,), (1,)), ((), ()))
NX = 4
NY = 4
NV = 2 * NX


def remote(src, dst, send_sem, recv_sem, lvl, col):
    return pltpu.make_async_remote_copy(
        src_ref=src,
        dst_ref=dst,
        send_sem=send_sem,
        recv_sem=recv_sem,
        device_id=(lvl, col),
        device_id_type=MESH,
    )


def arrived(dst, sem):
    pltpu.make_async_copy(dst, dst, sem).wait()


def kernel(
    nodes,
    rhs_ref,
    panel_ref,
    inverse_ref,
    pattern_ref,
    sample_ref,
    answer_ref,
    factor,
    inv,
    turned,
    rhs_in,
    rhs_all,
    first_in,
    later_in,
    push,
    sample_t,
    total,
    piece_out,
    sample_in,
    parent_in,
    above,
    part_out,
    own_in,
    solved_out,
    solved_in,
    gx_send,
    gx_recv,
    gy_send,
    gy_recv,
    rhs_send,
    rhs_recv,
    row_send,
    row_recv,
    up0_send,
    up0_recv,
    up_send,
    up_recv,
    down0_send,
    down0_recv,
    down_send,
    down_recv,
    own_send,
    own_recv,
    sample_send,
    sample_recv,
    solved_send,
    solved_recv,
):
    rows = rhs_ref.shape[0]
    width = inv.shape[1]
    slots = panel_ref.shape[0]
    tiles = pattern_ref.shape[2]
    tile = width // tiles
    span = NV * rows
    half = span // 2
    few = rhs_ref.shape[1] // NV

    s = lax.axis_index("lvl")
    c = lax.axis_index("col")
    y, v = c // NV, c % NV
    x, core = v // 2, v % 2
    other = 1 - core
    xp, xm, xo = (x + 1) % NX, (x + 3) % NX, (x + 2) % NX
    yp, ym, yo = (y + 1) % NY, (y + 3) % NY, (y + 2) % NY

    level = 0
    step = 1
    for e in range(1, slots + 1):
        whole = 1 - ((s + 1) % 2**e + 2**e - 1) // 2**e
        level = level + whole
        step = step + whole * 2 ** (e - 1)
    side = (s // (2 * step)) % 2
    parent = (s + step * (1 - 2 * side)) % nodes
    left = (s + nodes - step // 2) % nodes
    right = (s + step // 2) % nodes
    is_root = s == nodes - 1
    has_parent = s != nodes - 1
    has_left = s % 2 == 1
    has_right = jnp.logical_and(s % 2 == 1, s != nodes - 1)
    not_root = 1 - (s + 1) // nodes
    inner = s % 2

    def chip(yy, xx, cc):
        return (yy * NX + xx) * 2 + cc

    def mult(value, by):
        return pl.multiple_of(value, by)

    own_span = pl.ds(mult(y * span, 128), span)

    barrier = pltpu.get_barrier_semaphore()

    def greet(lvl, col):
        pl.semaphore_signal(barrier, inc=1, device_id=(lvl, col), device_id_type=MESH)

    for d in range(1, NV):
        greet(s, y * NV + (v + d) % NV)
    for d in range(1, NY):
        greet(s, (y + d) % NY * NV + v)

    @pl.when(has_parent)
    def _():
        for w in range(NY):
            greet(parent, w * NV + v)

    @pl.when(has_left)
    def _():
        for w in range(NY):
            greet(left, w * NV + v)

    @pl.when(has_right)
    def _():
        for w in range(NY):
            greet(right, w * NV + v)

    own_rows = pl.ds(mult(v * rows, 16), rows)
    inv[pl.ds(mult(c * rows, 16), rows), :] = inverse_ref[...]
    piece = 16

    def mask_slot(k):
        for q in range(rows // piece):
            tile_row = (c * rows + q * piece) // tile
            for j in range(tiles):
                keep = pattern_ref[k, tile_row, j].astype(jnp.float32)
                block = panel_ref[k, q * piece : (q + 1) * piece, j * tile : (j + 1) * tile]
                kept = (block.astype(jnp.float32) * keep).astype(jnp.bfloat16)
                factor[
                    k,
                    pl.ds(mult(v * rows + q * piece, 16), piece),
                    j * tile : (j + 1) * tile,
                ] = kept

    mask_slot(0)
    padded = jnp.concatenate(
        [rhs_ref[...], jnp.zeros((128 - rows, rhs_ref.shape[1]), jnp.float32)], axis=0
    )
    turned[...] = padded.T.reshape(NV, few, 128)
    rhs_in[v] = turned[v]

    @pl.when(s % 2 == 0)
    def _():
        first_in[0] = jnp.zeros_like(first_in[0])
        later_in[...] = jnp.zeros_like(later_in)

    @pl.when(jnp.logical_or(s % 2 == 0, is_root))
    def _():
        first_in[1] = jnp.zeros_like(first_in[1])

    pl.semaphore_wait(barrier, NV - 1 + NY - 1 + NY * (not_root + inner + inner * not_root))

    def block(g, xx, cc, lo, hi):
        if g == 0:
            start = mult(y * span + (2 * xx + cc) * rows, 16)
            return inv.at[pl.ds(start, rows), lo:hi]
        return factor.at[g - 1, pl.ds(mult((2 * xx + cc) * rows, 16), rows), lo:hi]

    mid = width // 2

    def gx_copy(g, i):
        ref, col = (
            lambda: (block(g, x, core, 0, width), chip(y, xp, core)),
            lambda: (block(g, x, core, 0, width), chip(y, xm, core)),
            lambda: (block(g, xm, core, 0, mid), chip(y, xp, core)),
            lambda: (block(g, xp, core, mid, width), chip(y, xm, core)),
            lambda: (block(g, x, core, 0, width), chip(y, x, other)),
            lambda: (block(g, xm, core, 0, width), chip(y, x, other)),
            lambda: (block(g, xp, core, 0, width), chip(y, x, other)),
            lambda: (block(g, xo, core, 0, width), chip(y, x, other)),
        )[i]()
        return remote(ref, ref, gx_send.at[g, i], gx_recv.at[g, i], s, col)

    def gx_wait(g, i):
        ref = (
            lambda: block(g, xm, core, 0, width),
            lambda: block(g, xp, core, 0, width),
            lambda: block(g, xo, core, 0, mid),
            lambda: block(g, xo, core, mid, width),
            lambda: block(g, x, other, 0, width),
            lambda: block(g, xm, other, 0, width),
            lambda: block(g, xp, other, 0, width),
            lambda: block(g, xo, other, 0, width),
        )[i]()
        arrived(ref, gx_recv.at[g, i])

    def gx_start(g):
        for i in (0, 1, 4):
            gx_copy(g, i).start()

    def gx_relay(g):
        gx_wait(g, 0)
        gx_copy(g, 2).start()
        gx_copy(g, 5).start()
        gx_wait(g, 1)
        gx_copy(g, 3).start()
        gx_copy(g, 6).start()

    def gx_last(g):
        gx_wait(g, 2)
        gx_wait(g, 3)
        gx_copy(g, 7).start()

    def gx_finish(g):
        for i in (4, 5, 6, 7):
            gx_wait(g, i)

    def stripe(yy, cc, lo, hi):
        return inv.at[pl.ds(mult(yy * span + cc * half + lo, 16), hi - lo), :]

    cut = half // 2

    def gy_copy(i):
        ref, col = (
            lambda: (stripe(y, core, 0, half), chip(yp, x, core)),
            lambda: (stripe(y, core, 0, half), chip(ym, x, core)),
            lambda: (stripe(ym, core, 0, cut), chip(yp, x, core)),
            lambda: (stripe(yp, core, cut, half), chip(ym, x, core)),
            lambda: (stripe(ym, core, 0, half), chip(y, x, other)),
            lambda: (stripe(yp, core, 0, half), chip(y, x, other)),
            lambda: (stripe(yo, core, 0, half), chip(y, x, other)),
        )[i]()
        return remote(ref, ref, gy_send.at[i], gy_recv.at[i], s, col)

    def gy_wait(i):
        ref = (
            lambda: stripe(ym, core, 0, half),
            lambda: stripe(yp, core, 0, half),
            lambda: stripe(yo, core, 0, cut),
            lambda: stripe(yo, core, cut, half),
            lambda: stripe(ym, other, 0, half),
            lambda: stripe(yp, other, 0, half),
            lambda: stripe(yo, other, 0, half),
        )[i]()
        arrived(ref, gy_recv.at[i])

    def rhs_copy(d):
        to = (v + d) % NV
        return remote(turned.at[to], rhs_in.at[v], rhs_send.at[d], rhs_recv.at[d], s, y * NV + to)

    def row_copy(d):
        ref = rhs_all.at[:, own_span]
        return remote(ref, ref, row_send.at[d], row_recv.at[d], s, (y + d) % NY * NV + v)

    gx_start(0)
    for d in range(1, NV):
        rhs_copy(d).start()
    gx_start(1)
    for k in range(1, slots):
        mask_slot(k)
    gx_relay(0)
    gx_last(0)
    gx_finish(0)
    gy_copy(0).start()
    gy_copy(1).start()

    for d in range(1, NV):
        arrived(rhs_in.at[(v + NV - d) % NV], rhs_recv.at[d])
    lane = lax.broadcasted_iota(jnp.int32, (few, 128), 1)
    joined = [jnp.zeros((few, 128), jnp.float32) for _ in range(span // 128)]
    for q in range(NV):
        a, b = divmod(q * rows, 128)
        moved = pltpu.roll(rhs_in[q], b, axis=1) if b else rhs_in[q]
        if b + rows <= 128:
            joined[a] = joined[a] + moved
        else:
            joined[a] = joined[a] + jnp.where(lane >= b, moved, 0.0)
            joined[a + 1] = joined[a + 1] + jnp.where(lane >= b, 0.0, moved)
    rhs_all[:, own_span] = jnp.concatenate(joined, axis=1)
    for d in range(1, NY):
        row_copy(d).start()

    gx_relay(1)
    gx_last(1)
    if slots > 1:
        gx_start(2)
    gx_finish(1)
    gy_wait(0)
    gy_copy(2).start()
    gy_copy(4).start()
    gy_wait(1)
    gy_copy(3).start()
    gy_copy(5).start()
    if slots > 1:
        gx_relay(2)
        gx_last(2)
        if slots > 2:
            gx_start(3)
    gy_wait(2)
    gy_wait(3)
    gy_copy(6).start()
    for d in range(1, NY):
        arrived(
            rhs_all.at[:, pl.ds(mult((y + NY - d) % NY * span, 128), span)], row_recv.at[d]
        )
    for i in (4, 5, 6):
        gy_wait(i)

    def up0_copy(w):
        return remote(
            push.at[0],
            first_in.at[side, :, own_span],
            up0_send.at[w],
            up0_recv.at[side, y],
            parent,
            w * NV + v,
        )

    def up_copy(k):
        return remote(
            push.at[k],
            later_in.at[side, k - 1],
            up_send.at[k],
            up_recv.at[side, k - 1],
            parent,
            y * NV + v,
        )

    @pl.when(has_left)
    def _():
        for w in range(NY):
            arrived(first_in.at[0, :, w * span : (w + 1) * span], up0_recv.at[0, w])

    @pl.when(has_right)
    def _():
        for w in range(NY):
            arrived(first_in.at[1, :, w * span : (w + 1) * span], up0_recv.at[1, w])

    incoming = first_in[0].astype(jnp.float32) + first_in[1].astype(jnp.float32)
    residual = (rhs_all[...] - incoming).astype(jnp.bfloat16)
    for w in range(NY):
        to = (w + 1) * span
        sample_t[:, w * span : to] = jnp.dot(
            residual[:, :to], inv[:to, w * span : to], preferred_element_type=jnp.float32
        )
    sample_half = sample_t[...].astype(jnp.bfloat16)

    def pushed(k):
        out = lax.dot_general(sample_half, factor[k], NT, preferred_element_type=jnp.float32)
        if k < slots - 1:

            @pl.when(has_left)
            def _():
                for i in range(2):
                    arrived(later_in.at[i, k], up_recv.at[i, k])

            out = out + later_in[0, k].astype(jnp.float32) + later_in[1, k].astype(jnp.float32)
        push[k] = out.astype(jnp.bfloat16)

    @pl.when(has_parent)
    def _():
        pushed(0)
        for w in range(NY):
            up0_copy(w).start()

    for k in range(1, slots):
        if k > 1:
            gx_relay(k + 1)
            gx_last(k + 1)
            if k + 2 <= slots:
                gx_start(k + 2)
        gx_finish(k + 1)

        @pl.when(level + k < slots)
        def _():
            pushed(k)
            up_copy(k).start()

    def cut_pieces(ref, value):
        parts = [value[:, 128 * a : 128 * (a + 1)] for a in range(span // 128)]
        for q in range(NV):
            a, b = divmod(q * rows, 128)
            moved = pltpu.roll(parts[a], 128 - b, axis=1) if b else parts[a]
            if b + rows > 128:
                after = pltpu.roll(parts[a + 1], 128 - b, axis=1)
                moved = jnp.where(lane < 128 - b, moved, after)
            ref[q] = moved

    def sample_copy(d):
        to = (v + d) % NV
        return remote(
            piece_out.at[to], sample_in.at[v], sample_send.at[d], sample_recv.at[d], s, y * NV + to
        )

    def solved_copy(d):
        to = (v + d) % NV
        return remote(
            solved_out.at[to], solved_in.at[v], solved_send.at[d], solved_recv.at[d], s, y * NV + to
        )

    cut_pieces(piece_out, sample_t[:, own_span])
    sample_in[v] = piece_out[v]
    for d in range(1, NV):
        sample_copy(d).start()

    def down_copy(k, child, i):
        return remote(
            above.at[k],
            above.at[k + 1],
            down_send.at[i, k],
            down_recv.at[k + 1],
            child,
            y * NV + v,
        )

    def down0_copy(w, child, i):
        return remote(
            part_out.at[w],
            parent_in.at[y],
            down0_send.at[i, w],
            down0_recv.at[y],
            child,
            w * NV + v,
        )

    def own_copy(d):
        to = (y + d) % NY
        return remote(part_out.at[to], own_in.at[y], own_send.at[d], own_recv.at[d], s, to * NV + v)

    def hand_down(k):
        @pl.when(has_left)
        def _():
            down_copy(k, left, 0).start()

        @pl.when(has_right)
        def _():
            down_copy(k, right, 1).start()

    group = lax.broadcasted_iota(jnp.int32, (few, width), 1) // span
    total[...] = jnp.where(group == y, sample_t[...], 0.0)
    for k in range(slots - 1, 0, -1):

        @pl.when(level + k < slots)
        def _():
            arrived(above.at[k], down_recv.at[k])
            if k < slots - 1:
                hand_down(k)
            total[...] -= jnp.dot(above[k], factor[k], preferred_element_type=jnp.float32)

    @pl.when(has_parent)
    def _():
        for w in range(NY):
            arrived(parent_in.at[w], down0_recv.at[w])
        summed = parent_in[0].astype(jnp.float32)
        for w in range(1, NY):
            summed = summed + parent_in[w].astype(jnp.float32)
        above[0] = summed.astype(jnp.bfloat16)
        total[...] -= jnp.dot(above[0], factor[0], preferred_element_type=jnp.float32)

    back = total[...].astype(jnp.bfloat16)
    for w in range(NY):
        start = w * span
        part = lax.dot_general(
            back[:, start:],
            inv[start : start + span, start:],
            NT,
            preferred_element_type=jnp.float32,
        )
        part_out[w] = part.astype(jnp.bfloat16)

        @pl.when(has_left)
        def _():
            down0_copy(w, left, 0).start()

        @pl.when(has_right)
        def _():
            down0_copy(w, right, 1).start()

    own_in[y] = part_out[y]
    for d in range(1, NY):
        own_copy(d).start()

    @pl.when(has_parent)
    def _():
        if slots > 1:
            hand_down(0)

    for d in range(1, NV):
        arrived(sample_in.at[(v + NV - d) % NV], sample_recv.at[d])
    sample_ref[...] = sample_in[...].reshape(NV * few, 128).T[:rows, :]

    for d in range(1, NY):
        arrived(own_in.at[(y + NY - d) % NY], own_recv.at[d])
    solved = own_in[0].astype(jnp.float32)
    for w in range(1, NY):
        solved = solved + own_in[w].astype(jnp.float32)
    cut_pieces(solved_out, solved)
    solved_in[v] = solved_out[v]
    for d in range(1, NV):
        solved_copy(d).start()
    for d in range(1, NV):
        arrived(solved_in.at[(v + NV - d) % NV], solved_recv.at[d])
    answer_ref[...] = solved_in[...].reshape(NV * few, 128).T[:rows, :]

    for g in range(slots + 1):
        for i in range(8):
            gx_copy(g, i).wait_send()
    for i in range(7):
        gy_copy(i).wait_send()
    for d in range(1, NV):
        rhs_copy(d).wait_send()
        sample_copy(d).wait_send()
        solved_copy(d).wait_send()
    for d in range(1, NY):
        row_copy(d).wait_send()
        own_copy(d).wait_send()

    @pl.when(has_parent)
    def _():
        for w in range(NY):
            up0_copy(w).wait_send()

    for k in range(1, slots):

        @pl.when(level + k < slots)
        def _():
            up_copy(k).wait_send()

    for i, (cond, child) in enumerate(((has_left, left), (has_right, right))):

        @pl.when(cond)
        def _():
            for w in range(NY):
                down0_copy(w, child, i).wait_send()

        for k in range(slots - 1):

            @pl.when(jnp.logical_and(cond, level + k < slots))
            def _():
                down_copy(k, child, i).wait_send()


def on_device(nodes, rhs, panel, inverse_t, pattern):
    rows, count = rhs.shape[1:]
    slots = panel.shape[1]
    width = inverse_t.shape[2]
    span = NV * rows
    few = count // NV
    f32, bf16 = jnp.float32, jnp.bfloat16
    dma = pltpu.SemaphoreType.DMA
    vmem = pl.BlockSpec(memory_space=pltpu.VMEM)
    outs = pl.pallas_call(
        functools.partial(kernel, nodes),
        out_shape=[jax.ShapeDtypeStruct((rows, count), f32)] * 2,
        in_specs=[vmem, vmem, vmem, pl.BlockSpec(memory_space=pltpu.SMEM)],
        out_specs=[vmem, vmem],
        scratch_shapes=[
            pltpu.VMEM((slots, span, width), bf16),
            pltpu.VMEM((width, width), bf16),
            pltpu.VMEM((NV, few, 128), f32),
            pltpu.VMEM((NV, few, 128), f32),
            pltpu.VMEM((few, width), f32),
            pltpu.VMEM((2, few, width), bf16),
            pltpu.VMEM((2, max(slots - 1, 1), few, span), bf16),
            pltpu.VMEM((slots, few, span), bf16),
            pltpu.VMEM((few, width), f32),
            pltpu.VMEM((few, width), f32),
            pltpu.VMEM((NV, few, 128), f32),
            pltpu.VMEM((NV, few, 128), f32),
            pltpu.VMEM((NY, few, span), bf16),
            pltpu.VMEM((slots, few, span), bf16),
            pltpu.VMEM((NY, few, span), bf16),
            pltpu.VMEM((NY, few, span), bf16),
            pltpu.VMEM((NV, few, 128), f32),
            pltpu.VMEM((NV, few, 128), f32),
        ]
        + [dma((slots + 1, 8))] * 2
        + [dma((7,))] * 2
        + [dma((NV,))] * 2
        + [dma((NY,))] * 2
        + [dma((NY,)), dma((2, NY))]
        + [dma((slots,)), dma((2, slots))]
        + [dma((2, NY)), dma((NY,))]
        + [dma((2, slots)), dma((slots,))]
        + [dma((NY,))] * 2
        + [dma((NV,))] * 4,
        compiler_params=pltpu.CompilerParams(
            collective_id=0, has_side_effects=True, vmem_limit_bytes=40 * 2**20
        ),
    )(rhs[0], panel[0], inverse_t[0], pattern[0])
    return outs[0][None], outs[1][None]


def solution(mesh):
    in_specs = (
        P("lvl", "col", None),
        P("lvl", None, "col", None),
        P("lvl", "col", None),
        P("lvl", None, None, None),
    )
    out_specs = (P("lvl", "col", None), P("lvl", "col", None))
    return jax.shard_map(
        functools.partial(on_device, mesh.shape["lvl"]),
        mesh=mesh,
        in_specs=in_specs,
        out_specs=out_specs,
        check_vma=False,
    )
```

```python
import functools

import jax
import jax.numpy as jnp
from jax import lax
from jax.experimental import pallas as pl
from jax.experimental.pallas import tpu as pltpu
from jax.sharding import PartitionSpec as P

MESH = pl.DeviceIdType.MESH
NT = (((1,), (1,)), ((), ()))
NX = 4
NY = 4
NV = 2 * NX
ORDER = (1, 3, 2)


def remote(src, dst, send_sem, recv_sem, lvl, col):
    return pltpu.make_async_remote_copy(
        src_ref=src,
        dst_ref=dst,
        send_sem=send_sem,
        recv_sem=recv_sem,
        device_id=(lvl, col),
        device_id_type=MESH,
    )


def arrived(dst, sem):
    pltpu.make_async_copy(dst, dst, sem).wait()


def kernel(
    nodes,
    rhs_ref,
    panel_ref,
    inverse_ref,
    pattern_ref,
    sample_ref,
    answer_ref,
    factor,
    inv,
    top_inv,
    turned,
    rhs_in,
    rhs_all,
    top_rhs,
    first_in,
    later_in,
    push,
    shares,
    sample_t,
    total,
    piece_out,
    sample_in,
    parent_in,
    above,
    part_out,
    own_in,
    solved_out,
    solved_in,
    top_piece,
    gx_send,
    gx_recv,
    gy_send,
    gy_recv,
    gs_send,
    gs_recv,
    rhs_send,
    rhs_recv,
    row_send,
    row_recv,
    share_send,
    share_recv,
    up0_send,
    up0_recv,
    up_send,
    up_recv,
    down0_send,
    down0_recv,
    down_send,
    down_recv,
    own_send,
    own_recv,
    sample_send,
    sample_recv,
    solved_send,
    solved_recv,
    move_send,
    move_recv,
    top_send,
):
    rows = rhs_ref.shape[0]
    width = inv.shape[-1]
    slots = panel_ref.shape[0]
    tiles = pattern_ref.shape[2]
    tile = width // tiles
    span = NV * rows
    few = rhs_ref.shape[1] // NV
    f32, bf16 = jnp.float32, jnp.bfloat16
    root, top = nodes - 1, nodes // 2 - 1

    s = lax.axis_index("lvl")
    c = lax.axis_index("col")
    y, v = c // NV, c % NV
    x, core = v // 2, v % 2
    other = 1 - core

    level = 0
    step = 1
    for e in range(1, slots + 1):
        whole = 1 - ((s + 1) % 2**e + 2**e - 1) // 2**e
        level = level + whole
        step = step + whole * 2 ** (e - 1)
    side = (s // (2 * step)) % 2
    parent = (s + step * (1 - 2 * side)) % nodes
    left = (s + nodes - step // 2) % nodes
    right = (s + step // 2) % nodes
    one_root = (s + 1) // nodes
    one_top = (level + 1) // slots - one_root
    inner = s % 2
    is_root = one_root == 1
    is_top = one_top == 1
    not_root = one_root == 0
    is_leaf = inner == 0
    has_kids = inner * (1 - one_root) == 1
    has_parent = one_root + one_top == 0

    def chip(yy, xx, cc):
        return (yy * NX + xx) * 2 + cc

    own_span = pl.ds(pl.multiple_of(y * span, 128), span)

    barrier = pltpu.get_barrier_semaphore()

    def greet(lvl, col):
        pl.semaphore_signal(barrier, inc=1, device_id=(lvl, col), device_id_type=MESH)

    for d in range(1, NV):
        greet(s, y * NV + (v + d) % NV)
    for d in range(1, NY):
        greet(s, (y + d) % NY * NV + v)

    @pl.when(has_parent)
    def _():
        for w in range(NY):
            greet(parent, w * NV + v)

    @pl.when(has_kids)
    def _():
        for w in range(NY):
            greet(left, w * NV + v)
            greet(right, w * NV + v)

    @pl.when(is_top)
    def _():
        for q in range(NV):
            greet(root, y * NV + q)

    @pl.when(is_root)
    def _():
        for q in range(NV):
            greet(top, y * NV + q)

    inv[y, x, core] = inverse_ref[...]
    piece = 16

    def mask_slot(k):
        for q in range(rows // piece):
            tile_row = (c * rows + q * piece) // tile
            for j in range(tiles):
                keep = pattern_ref[k, tile_row, j].astype(f32)
                part = (slice(q * piece, (q + 1) * piece), slice(j * tile, (j + 1) * tile))
                block = panel_ref[(k,) + part]
                factor[(k, x, core) + part] = (block.astype(f32) * keep).astype(bf16)

    padded = jnp.concatenate(
        [rhs_ref[...], jnp.zeros((128 - rows, rhs_ref.shape[1]), f32)], axis=0
    )
    turned[...] = padded.T.reshape(NV, few, 128)
    rhs_in[v] = turned[v]
    mask_slot(0)

    pl.semaphore_wait(
        barrier,
        NV - 1
        + NY - 1
        + NY * (1 - one_root - one_top)
        + 2 * NY * inner * (1 - one_root)
        + NV * (one_top + one_root),
    )

    last = slots + 1

    def block(g, xx, cc):
        if g == 0:
            return inv.at[y, xx, cc]
        if g == last:
            return top_inv.at[xx, cc]
        return factor.at[g - 1, xx, cc]

    def gx_copy(g, i):
        if i == 0:
            ref, col = block(g, x, core), chip(y, x, other)
        elif i < NX:
            ref, col = block(g, x, core), chip(y, (x + i) % NX, core)
        else:
            ref, col = block(g, (x + 2 * NX - 1 - i) % NX, core), chip(y, x, other)
        return remote(ref, ref, gx_send.at[g, i], gx_recv.at[g, i], s, col)

    def gx_wait(g, i):
        if i == 0:
            ref = block(g, x, other)
        elif i < NX:
            ref = block(g, (x + NX - i) % NX, core)
        else:
            ref = block(g, (x + 2 * NX - 1 - i) % NX, other)
        arrived(ref, gx_recv.at[g, i])

    def gx_start(g):
        for i in ORDER + (0,):
            gx_copy(g, i).start()

    def gx_pass(g, then=None):
        for i in ORDER:
            gx_wait(g, i)
            gx_copy(g, i + NX - 1).start()
            if then is not None:
                then(i)

    def gx_finish(g):
        for i in (0,) + tuple(i + NX - 1 for i in ORDER):
            gx_wait(g, i)

    def each_y(body):
        for yy in range(NY):

            @pl.when(y == yy)
            def _(yy=yy):
                body(yy)

    def gy_copy(yy, d, j):
        ref = inv.at[yy, (x + j) % NX, core, :, yy * span :]
        col = chip((yy + d) % NY, x, core)
        return remote(ref, ref, gy_send.at[d, j], gy_recv.at[d, j], s, col)

    def gs_copy(yy, d):
        source = (yy + NY - d) % NY
        ref = inv.at[source, :, core, :, source * span :]
        return remote(ref, ref, gs_send.at[d], gs_recv.at[d], s, chip(yy, x, other))

    def gy_start(j):
        def body(yy):
            for d in ORDER:
                gy_copy(yy, d, j).start()

        each_y(body)

    def gy_pass():
        def body(yy):
            for d in ORDER:
                source = (yy + NY - d) % NY
                for j in range(NX):
                    arrived(
                        inv.at[source, (x + j) % NX, core, :, source * span :], gy_recv.at[d, j]
                    )
                gs_copy(yy, d).start()

        each_y(body)

    def gy_finish():
        def body(yy):
            for d in ORDER:
                source = (yy + NY - d) % NY
                arrived(inv.at[source, :, other, :, source * span :], gs_recv.at[d])

        each_y(body)

    def rhs_copy(d):
        to = (v + d) % NV
        return remote(turned.at[to], rhs_in.at[v], rhs_send.at[d], rhs_recv.at[d], s, y * NV + to)

    def row_copy(d):
        ref = rhs_all.at[:, own_span]
        return remote(ref, ref, row_send.at[d], row_recv.at[d], s, (y + d) % NY * NV + v)

    lane = lax.broadcasted_iota(jnp.int32, (few, 128), 1)

    def join_rhs():
        for d in range(1, NV):
            arrived(rhs_in.at[(v + NV - d) % NV], rhs_recv.at[d])
        joined = [jnp.zeros((few, 128), f32) for _ in range(span // 128)]
        for q in range(NV):
            a, b = divmod(q * rows, 128)
            moved = pltpu.roll(rhs_in[q], b, axis=1) if b else rhs_in[q]
            if b + rows <= 128:
                joined[a] = joined[a] + moved
            else:
                joined[a] = joined[a] + jnp.where(lane >= b, moved, 0.0)
                joined[a + 1] = joined[a + 1] + jnp.where(lane >= b, 0.0, moved)
        rhs_all[:, own_span] = jnp.concatenate(joined, axis=1)

    def share_copy(d):
        ref = shares.at[y]
        return remote(ref, ref, share_send.at[d], share_recv.at[d], s, (y + d) % NY * NV + v)

    def share_start(residual, rows_of):
        product = jnp.dot(residual, rows_of.reshape(span, width), preferred_element_type=f32)
        shares[y] = product.astype(bf16)
        for d in ORDER:
            share_copy(d).start()

    def share_sum():
        for d in ORDER:
            arrived(shares.at[(y + NY - d) % NY], share_recv.at[d])
        summed = shares[0].astype(f32)
        for w in range(1, NY):
            summed = summed + shares[w].astype(f32)
        return summed

    def up0_copy(w):
        return remote(
            push.at[0],
            first_in.at[side, :, own_span],
            up0_send.at[w],
            up0_recv.at[side, y],
            parent,
            w * NV + v,
        )

    def up_copy(k):
        return remote(
            push.at[k],
            later_in.at[side, k - 1],
            up_send.at[k],
            up_recv.at[side, k - 1],
            parent,
            y * NV + v,
        )

    def flat(k):
        return factor[k].reshape(span, width)

    def pushed(k, sample_half):
        return lax.dot_general(sample_half, flat(k), NT, preferred_element_type=f32)

    def cut_pieces(ref, value):
        parts = [value[:, 128 * a : 128 * (a + 1)] for a in range(span // 128)]
        for q in range(NV):
            a, b = divmod(q * rows, 128)
            moved = pltpu.roll(parts[a], 128 - b, axis=1) if b else parts[a]
            if b + rows > 128:
                after = pltpu.roll(parts[a + 1], 128 - b, axis=1)
                moved = jnp.where(lane < 128 - b, moved, after)
            ref[q] = moved

    def sample_copy(d):
        to = (v + d) % NV
        return remote(
            piece_out.at[to], sample_in.at[v], sample_send.at[d], sample_recv.at[d], s, y * NV + to
        )

    def solved_copy(d):
        to = (v + d) % NV
        return remote(
            solved_out.at[to], solved_in.at[v], solved_send.at[d], solved_recv.at[d], s, y * NV + to
        )

    def top_copy(i, d):
        to = (v + d) % NV
        ref, sem = (sample_in, sample_recv) if i == 0 else (solved_in, solved_recv)
        return remote(
            top_piece.at[i, to], ref.at[v], top_send.at[i, d], sem.at[d], root, y * NV + to
        )

    def sample_out():
        cut_pieces(piece_out, sample_t[:, own_span])
        sample_in[v] = piece_out[v]
        for d in range(1, NV):
            sample_copy(d).start()

    def move_inv():
        return remote(
            inverse_ref, top_inv.at[x, core], move_send.at[0], move_recv.at[0], top, c
        )

    def move_rhs():
        return remote(
            rhs_all.at[:, own_span], top_rhs, move_send.at[1], move_recv.at[1], top, c
        )

    def down_copy(k, child, i):
        return remote(
            above.at[k],
            above.at[k + 1],
            down_send.at[i, k],
            down_recv.at[k + 1],
            child,
            y * NV + v,
        )

    def down0_copy(w, child, i):
        return remote(
            part_out.at[w],
            parent_in.at[y],
            down0_send.at[i, w],
            down0_recv.at[y],
            child,
            w * NV + v,
        )

    def own_copy(d):
        to = (y + d) % NY
        return remote(part_out.at[to], own_in.at[y], own_send.at[d], own_recv.at[d], s, to * NV + v)

    def hand_down(k):
        @pl.when(has_kids)
        def _():
            down_copy(k, left, 0).start()
            down_copy(k, right, 1).start()

    @pl.when(is_leaf)
    def _():
        gx_start(0)
        for d in range(1, NV):
            rhs_copy(d).start()
        for k in range(1, slots):
            mask_slot(k)
        gx_pass(0, lambda i: gx_start(1) if i == ORDER[0] else None)
        join_rhs()
        gx_finish(0)
        share_start(rhs_all[:, own_span].astype(bf16), inv[y])
        gx_pass(1, lambda i: gx_start(2) if i == ORDER[0] and slots > 1 else None)
        sample_t[...] = share_sum()
        sample_half = sample_t[...].astype(bf16)
        for k in range(slots):
            if k > 0:
                gx_pass(
                    k + 1, lambda i: gx_start(k + 2) if i == ORDER[0] and k + 2 <= slots else None
                )
            gx_finish(k + 1)
            push[k] = pushed(k, sample_half).astype(bf16)
            if k == 0:
                for w in range(NY):
                    up0_copy(w).start()
            else:
                up_copy(k).start()
        for j in range(NX):
            gy_start(j)
        sample_out()
        gy_pass()
        gy_finish()

    @pl.when(inner == 1)
    def _():
        @pl.when(is_root)
        def _():
            move_inv().start()

        @pl.when(not_root)
        def _():
            gx_start(0)
            gy_start(0)

        for d in range(1, NV):
            rhs_copy(d).start()
        for k in range(1, slots - 1):
            mask_slot(k)

        @pl.when(not_root)
        def _():
            def follow(i):
                gy_start(NX - i)
                if i == ORDER[0]:
                    gx_start(1)

            gx_pass(0, follow)

        join_rhs()

        @pl.when(is_root)
        def _():
            move_rhs().start()

        @pl.when(not_root)
        def _():
            for d in range(1, NY):
                row_copy(d).start()
            gx_pass(1)
            for k in range(1, slots - 1):

                @pl.when(level + k < slots)
                def _():
                    gx_start(k + 1)

            @pl.when(is_top)
            def _():
                arrived(top_inv.at[x, core], move_recv.at[0])
                gx_start(last)

            for k in range(1, slots - 1):

                @pl.when(level + k < slots)
                def _():
                    gx_pass(k + 1)

            @pl.when(is_top)
            def _():
                gx_pass(last)

            gy_pass()
            for d in range(1, NY):
                group_of = (y + NY - d) % NY
                arrived(
                    rhs_all.at[:, pl.ds(pl.multiple_of(group_of * span, 128), span)],
                    row_recv.at[d],
                )
            gx_finish(0)
            gx_finish(1)
            for k in range(1, slots - 1):

                @pl.when(level + k < slots)
                def _():
                    gx_finish(k + 1)

            @pl.when(is_top)
            def _():
                gx_finish(last)
                arrived(top_rhs, move_recv.at[1])

            gy_finish()

            for i in range(2):
                for w in range(NY):
                    arrived(first_in.at[i, :, w * span : (w + 1) * span], up0_recv.at[i, w])
            incoming = first_in[0].astype(f32) + first_in[1].astype(f32)
            residual = (rhs_all[...] - incoming).astype(bf16)
            for w in range(NY):
                to = (w + 1) * span
                sample_t[:, w * span : to] = jnp.dot(
                    residual[:, :to],
                    inv[: w + 1, :, :, :, w * span : to].reshape(to, span),
                    preferred_element_type=f32,
                )
            sample_half = sample_t[...].astype(bf16)

            def pushed_sum(k):
                out = pushed(k, sample_half)
                for i in range(2):
                    arrived(later_in.at[i, k], up_recv.at[i, k])
                return out + later_in[0, k].astype(f32) + later_in[1, k].astype(f32)

            @pl.when(has_parent)
            def _():
                push[0] = pushed_sum(0).astype(bf16)
                for w in range(NY):
                    up0_copy(w).start()

            @pl.when(is_top)
            def _():
                residual_root = (top_rhs[...] - pushed_sum(0)).astype(bf16)
                share_start(residual_root, top_inv[...])
                root_t = share_sum()
                total[...] = root_t
                solved_root = lax.dot_general(
                    root_t.astype(bf16),
                    top_inv[...].reshape(span, width),
                    NT,
                    preferred_element_type=f32,
                )
                above[0] = solved_root.astype(bf16)
                down_copy(0, left, 0).start()
                down_copy(0, right, 1).start()
                cut_pieces(top_piece.at[1], solved_root)

            for k in range(1, slots - 1):

                @pl.when(level + k < slots)
                def _():
                    push[k] = pushed_sum(k).astype(bf16)
                    up_copy(k).start()

            @pl.when(level + 1 < slots)
            def _():
                sample_out()

    @pl.when(not_root)
    def _():
        group = lax.broadcasted_iota(jnp.int32, (few, width), 1) // span

        @pl.when(is_top)
        def _():
            cut_pieces(top_piece.at[0], total[:, own_span])

        total[...] = jnp.where(group == y, sample_t[...], 0.0)
        for k in range(slots - 1, 0, -1):

            @pl.when(level + k < slots)
            def _():
                arrived(above.at[k], down_recv.at[k])
                if k < slots - 1:
                    hand_down(k)
                total[...] -= jnp.dot(above[k], flat(k), preferred_element_type=f32)

        @pl.when(has_parent)
        def _():
            for w in range(NY):
                arrived(parent_in.at[w], down0_recv.at[w])
            summed = parent_in[0].astype(f32)
            for w in range(1, NY):
                summed = summed + parent_in[w].astype(f32)
            above[0] = summed.astype(bf16)

        total[...] -= jnp.dot(above[0], flat(0), preferred_element_type=f32)

        back = total[...].astype(bf16)
        for w in range(NY):
            start = w * span
            part = lax.dot_general(
                back[:, start:],
                inv[w, :, :, :, start:].reshape(span, width - start),
                NT,
                preferred_element_type=f32,
            )
            part_out[w] = part.astype(bf16)

            @pl.when(has_kids)
            def _():
                down0_copy(w, left, 0).start()
                down0_copy(w, right, 1).start()

        own_in[y] = part_out[y]
        for d in ORDER:
            own_copy(d).start()

        @pl.when(has_parent)
        def _():
            if slots > 1:
                hand_down(0)

        @pl.when(is_top)
        def _():
            for d in range(NV):
                top_copy(0, d).start()
                top_copy(1, d).start()
            sample_out()

        for d in range(1, NV):
            arrived(sample_in.at[(v + NV - d) % NV], sample_recv.at[d])
        sample_ref[...] = sample_in[...].reshape(NV * few, 128).T[:rows, :]

        for d in ORDER:
            arrived(own_in.at[(y + NY - d) % NY], own_recv.at[d])
        solved = own_in[0].astype(f32)
        for w in range(1, NY):
            solved = solved + own_in[w].astype(f32)
        cut_pieces(solved_out, solved)
        solved_in[v] = solved_out[v]
        for d in range(1, NV):
            solved_copy(d).start()
        for d in range(1, NV):
            arrived(solved_in.at[(v + NV - d) % NV], solved_recv.at[d])
        answer_ref[...] = solved_in[...].reshape(NV * few, 128).T[:rows, :]

    @pl.when(is_root)
    def _():
        for d in range(NV):
            arrived(sample_in.at[(v + NV - d) % NV], sample_recv.at[d])
            arrived(solved_in.at[(v + NV - d) % NV], solved_recv.at[d])
        sample_ref[...] = sample_in[...].reshape(NV * few, 128).T[:rows, :]
        answer_ref[...] = solved_in[...].reshape(NV * few, 128).T[:rows, :]

    for d in range(1, NV):
        rhs_copy(d).wait_send()

    def gx_sent(g):
        for i in range(2 * NX - 1):
            gx_copy(g, i).wait_send()

    @pl.when(is_root)
    def _():
        move_inv().wait_send()
        move_rhs().wait_send()

    @pl.when(not_root)
    def _():
        gx_sent(0)
        for k in range(slots):

            @pl.when(level + k < slots)
            def _():
                gx_sent(k + 1)

        def gy_sent(yy):
            for d in ORDER:
                for j in range(NX):
                    gy_copy(yy, d, j).wait_send()
                gs_copy(yy, d).wait_send()

        each_y(gy_sent)
        for d in range(1, NV):
            sample_copy(d).wait_send()
            solved_copy(d).wait_send()
        for d in ORDER:
            own_copy(d).wait_send()

    @pl.when(has_kids)
    def _():
        for d in range(1, NY):
            row_copy(d).wait_send()
        for i, child in enumerate((left, right)):
            for w in range(NY):
                down0_copy(w, child, i).wait_send()
            for k in range(slots - 1):

                @pl.when(level + k < slots)
                def _():
                    down_copy(k, child, i).wait_send()

    @pl.when(has_parent)
    def _():
        for w in range(NY):
            up0_copy(w).wait_send()
        for k in range(1, slots):

            @pl.when(level + k < slots)
            def _():
                up_copy(k).wait_send()

    def share_sent():
        for d in ORDER:
            share_copy(d).wait_send()

    @pl.when(is_leaf)
    def _():
        share_sent()

    @pl.when(is_top)
    def _():
        share_sent()
        gx_sent(last)
        for d in range(NV):
            top_copy(0, d).wait_send()
            top_copy(1, d).wait_send()


def on_device(nodes, rhs, panel, inverse_t, pattern):
    rows, count = rhs.shape[1:]
    slots = panel.shape[1]
    width = inverse_t.shape[2]
    span = NV * rows
    few = count // NV
    f32, bf16 = jnp.float32, jnp.bfloat16
    dma = pltpu.SemaphoreType.DMA
    vmem = pl.BlockSpec(memory_space=pltpu.VMEM)
    outs = pl.pallas_call(
        functools.partial(kernel, nodes),
        out_shape=[jax.ShapeDtypeStruct((rows, count), f32)] * 2,
        in_specs=[vmem, vmem, vmem, pl.BlockSpec(memory_space=pltpu.SMEM)],
        out_specs=[vmem, vmem],
        scratch_shapes=[
            pltpu.VMEM((slots, NX, 2, rows, width), bf16),
            pltpu.VMEM((NY, NX, 2, rows, width), bf16),
            pltpu.VMEM((NX, 2, rows, width), bf16),
            pltpu.VMEM((NV, few, 128), f32),
            pltpu.VMEM((NV, few, 128), f32),
            pltpu.VMEM((few, width), f32),
            pltpu.VMEM((few, span), f32),
            pltpu.VMEM((2, few, width), bf16),
            pltpu.VMEM((2, max(slots - 1, 1), few, span), bf16),
            pltpu.VMEM((slots, few, span), bf16),
            pltpu.VMEM((NY, few, width), bf16),
            pltpu.VMEM((few, width), f32),
            pltpu.VMEM((few, width), f32),
            pltpu.VMEM((NV, few, 128), f32),
            pltpu.VMEM((NV, few, 128), f32),
            pltpu.VMEM((NY, few, span), bf16),
            pltpu.VMEM((slots, few, span), bf16),
            pltpu.VMEM((NY, few, span), bf16),
            pltpu.VMEM((NY, few, span), bf16),
            pltpu.VMEM((NV, few, 128), f32),
            pltpu.VMEM((NV, few, 128), f32),
            pltpu.VMEM((2, NV, few, 128), f32),
        ]
        + [dma((slots + 2, 2 * NX - 1))] * 2
        + [dma((NY, NX))] * 2
        + [dma((NY,))] * 2
        + [dma((NV,))] * 2
        + [dma((NY,))] * 2
        + [dma((NY,))] * 2
        + [dma((NY,)), dma((2, NY))]
        + [dma((slots,)), dma((2, slots))]
        + [dma((2, NY)), dma((NY,))]
        + [dma((2, slots)), dma((slots,))]
        + [dma((NY,))] * 2
        + [dma((NV,))] * 4
        + [dma((2,))] * 2
        + [dma((2, NV))],
        compiler_params=pltpu.CompilerParams(
            collective_id=0, has_side_effects=True, vmem_limit_bytes=40 * 2**20
        ),
    )(rhs[0], panel[0], inverse_t[0], pattern[0])
    return outs[0][None], outs[1][None]


def solution(mesh):
    in_specs = (
        P("lvl", "col", None),
        P("lvl", None, "col", None),
        P("lvl", "col", None),
        P("lvl", None, None, None),
    )
    out_specs = (P("lvl", "col", None), P("lvl", "col", None))
    return jax.shard_map(
        functools.partial(on_device, mesh.shape["lvl"]),
        mesh=mesh,
        in_specs=in_specs,
        out_specs=out_specs,
        check_vma=False,
    )
```

```python
import functools

import jax
import jax.numpy as jnp
from jax import lax
from jax.experimental import pallas as pl
from jax.experimental.pallas import tpu as pltpu
from jax.sharding import PartitionSpec as P

MESH = pl.DeviceIdType.MESH
NT = (((1,), (1,)), ((), ()))
NX = 4
NY = 4
NV = 2 * NX
ORDER = (1, 3, 2)


def remote(src, dst, send_sem, recv_sem, lvl, col):
    return pltpu.make_async_remote_copy(
        src_ref=src,
        dst_ref=dst,
        send_sem=send_sem,
        recv_sem=recv_sem,
        device_id=(lvl, col),
        device_id_type=MESH,
    )


def arrived(dst, sem):
    pltpu.make_async_copy(dst, dst, sem).wait()


def kernel(
    nodes,
    rhs_ref,
    panel_ref,
    inverse_ref,
    pattern_ref,
    sample_ref,
    answer_ref,
    rhs_own,
    panel_own,
    pattern_own,
    factor,
    inv,
    top_inv,
    turned,
    rhs_in,
    rhs_all,
    top_rhs,
    first_in,
    later_in,
    push,
    shares,
    sample_t,
    total,
    piece_out,
    sample_in,
    parent_in,
    above,
    part_out,
    own_in,
    solved_out,
    solved_in,
    top_piece,
    root_sample,
    root_solved,
    gx_send,
    gx_recv,
    gy_send,
    gy_recv,
    gs_send,
    gs_recv,
    rhs_send,
    rhs_recv,
    row_send,
    row_recv,
    share_send,
    share_recv,
    up0_send,
    up0_recv,
    up_send,
    up_recv,
    down0_send,
    down0_recv,
    down_send,
    down_recv,
    own_send,
    own_recv,
    sample_send,
    sample_recv,
    solved_send,
    solved_recv,
    move_send,
    move_recv,
    top_send,
    load_sem,
    joint,
    last_out,
    last_in,
    last_send,
    last_recv,
):
    rows = rhs_ref.shape[0]
    width = inv.shape[-1]
    slots = panel_ref.shape[0]
    tiles = pattern_ref.shape[2]
    tile = width // tiles
    span = NV * rows
    few = rhs_ref.shape[1] // NV
    f32, bf16 = jnp.float32, jnp.bfloat16
    root, top = nodes - 1, nodes // 2 - 1

    s = lax.axis_index("lvl")
    c = lax.axis_index("col")
    y, v = c // NV, c % NV
    x, core = v // 2, v % 2
    other = 1 - core

    level = 0
    step = 1
    for e in range(1, slots + 1):
        whole = 1 - ((s + 1) % 2**e + 2**e - 1) // 2**e
        level = level + whole
        step = step + whole * 2 ** (e - 1)
    side = (s // (2 * step)) % 2
    parent = (s + step * (1 - 2 * side)) % nodes
    left = (s + nodes - step // 2) % nodes
    right = (s + step // 2) % nodes
    one_root = (s + 1) // nodes
    one_top = (level + 1) // slots - one_root
    inner = s % 2
    is_root = one_root == 1
    is_top = one_top == 1
    not_root = one_root == 0
    is_leaf = inner == 0
    has_kids = inner * (1 - one_root) == 1
    has_parent = one_root + one_top == 0

    def chip(yy, xx, cc):
        return (yy * NX + xx) * 2 + cc

    own_span = pl.ds(pl.multiple_of(y * span, 128), span)

    barrier = pltpu.get_barrier_semaphore()

    def greet(lvl, col):
        pl.semaphore_signal(barrier, inc=1, device_id=(lvl, col), device_id_type=MESH)

    @pl.when(is_leaf)
    def _():
        for d in range(1, NY * NV):
            greet(s, (c + d) % (NY * NV))

    @pl.when(inner == 1)
    def _():
        for d in range(1, NV):
            greet(s, y * NV + (v + d) % NV)
        for d in range(1, NY):
            greet(s, (y + d) % NY * NV + v)

    @pl.when(has_parent)
    def _():
        for w in range(NY):
            greet(parent, w * NV + v)

    @pl.when(has_kids)
    def _():
        for w in range(NY):
            greet(left, w * NV + v)
            greet(right, w * NV + v)

    @pl.when(is_top)
    def _():
        for q in range(NV):
            greet(root, y * NV + q)

    @pl.when(is_root)
    def _():
        for q in range(NV):
            greet(top, y * NV + q)

    loads = (
        pltpu.make_async_copy(rhs_ref, rhs_own, load_sem.at[0]),
        pltpu.make_async_copy(inverse_ref, inv.at[y, x, core], load_sem.at[1]),
        pltpu.make_async_copy(pattern_ref, pattern_own, load_sem.at[2]),
        pltpu.make_async_copy(panel_ref, panel_own, load_sem.at[3]),
    )
    for load in loads:
        load.start()
    piece = 16

    def mask_slot(k):
        for q in range(rows // piece):
            tile_row = (c * rows + q * piece) // tile
            for j in range(tiles):
                keep = pattern_own[k, tile_row, j].astype(f32)
                part = (slice(q * piece, (q + 1) * piece), slice(j * tile, (j + 1) * tile))
                block = panel_own[(k,) + part]
                factor[(k, x, core) + part] = (block.astype(f32) * keep).astype(bf16)

    loads[0].wait()
    padded = jnp.concatenate(
        [rhs_own[...], jnp.zeros((128 - rows, rhs_ref.shape[1]), f32)], axis=0
    )
    turned[...] = padded.T.reshape(NV, few, 128)
    rhs_in[v] = turned[v]
    loads[1].wait()

    pl.semaphore_wait(
        barrier,
        (NV - 1 + NY - 1) * inner
        + (NV * NY - 1) * (1 - inner)
        + NY * (1 - one_root - one_top)
        + 2 * NY * inner * (1 - one_root)
        + NV * (one_top + one_root),
    )

    last = slots + 1

    def block(g, xx, cc):
        if g == 0:
            return inv.at[y, xx, cc]
        if g == last:
            return top_inv.at[xx, cc]
        return factor.at[g - 1, xx, cc]

    def gx_copy(g, i):
        if i == 0:
            ref, col = block(g, x, core), chip(y, x, other)
        elif i < NX:
            ref, col = block(g, x, core), chip(y, (x + i) % NX, core)
        else:
            ref, col = block(g, (x + 2 * NX - 1 - i) % NX, core), chip(y, x, other)
        return remote(ref, ref, gx_send.at[g, i], gx_recv.at[g, i], s, col)

    def gx_wait(g, i):
        if i == 0:
            ref = block(g, x, other)
        elif i < NX:
            ref = block(g, (x + NX - i) % NX, core)
        else:
            ref = block(g, (x + 2 * NX - 1 - i) % NX, other)
        arrived(ref, gx_recv.at[g, i])

    def gx_start(g):
        for i in ORDER + (0,):
            gx_copy(g, i).start()

    def gx_pass(g, then=None):
        for i in ORDER:
            gx_wait(g, i)
            gx_copy(g, i + NX - 1).start()
            if then is not None:
                then(NX - i)

    def gx_finish(g):
        for i in (0,) + tuple(i + NX - 1 for i in ORDER):
            gx_wait(g, i)

    def each_y(body):
        for yy in range(NY):

            @pl.when(y == yy)
            def _(yy=yy):
                body(yy)

    def gy_copy(yy, d, j):
        ref = inv.at[yy, (x + j) % NX, core, :, yy * span :]
        col = chip((yy + d) % NY, x, core)
        return remote(ref, ref, gy_send.at[d, j], gy_recv.at[d, j], s, col)

    def gs_copy(yy, d):
        source = (yy + NY - d) % NY
        ref = inv.at[source, :, core, :, source * span :]
        return remote(ref, ref, gs_send.at[d], gs_recv.at[d], s, chip(yy, x, other))

    def gy_start(j):
        def body(yy):
            for d in ORDER:
                gy_copy(yy, d, j).start()

        each_y(body)

    def gy_pass():
        def body(yy):
            for d in ORDER:
                source = (yy + NY - d) % NY
                for j in range(NX):
                    arrived(
                        inv.at[source, (x + j) % NX, core, :, source * span :], gy_recv.at[d, j]
                    )
                gs_copy(yy, d).start()

        each_y(body)

    def gy_finish():
        def body(yy):
            for d in ORDER:
                source = (yy + NY - d) % NY
                arrived(inv.at[source, :, other, :, source * span :], gs_recv.at[d])

        each_y(body)

    def rhs_copy(d):
        to = (v + d) % NV
        return remote(turned.at[to], rhs_in.at[v], rhs_send.at[d], rhs_recv.at[d], s, y * NV + to)

    def row_copy(d):
        ref = rhs_all.at[:, own_span]
        return remote(ref, ref, row_send.at[d], row_recv.at[d], s, (y + d) % NY * NV + v)

    lane = lax.broadcasted_iota(jnp.int32, (few, 128), 1)

    def join_rhs():
        for d in range(1, NV):
            arrived(rhs_in.at[(v + NV - d) % NV], rhs_recv.at[d])
        joined = [jnp.zeros((few, 128), f32) for _ in range(span // 128)]
        for q in range(NV):
            a, b = divmod(q * rows, 128)
            moved = pltpu.roll(rhs_in[q], b, axis=1) if b else rhs_in[q]
            if b + rows <= 128:
                joined[a] = joined[a] + moved
            else:
                joined[a] = joined[a] + jnp.where(lane >= b, moved, 0.0)
                joined[a + 1] = joined[a + 1] + jnp.where(lane >= b, 0.0, moved)
        rhs_all[:, own_span] = jnp.concatenate(joined, axis=1)

    def share_copy(d):
        ref = shares.at[y]
        return remote(ref, ref, share_send.at[d], share_recv.at[d], s, (y + d) % NY * NV + v)

    def share_start(residual, rows_of):
        product = jnp.dot(residual, rows_of.reshape(span, width), preferred_element_type=f32)
        shares[y] = product.astype(bf16)
        for d in ORDER:
            share_copy(d).start()

    def share_sum():
        for d in ORDER:
            arrived(shares.at[(y + NY - d) % NY], share_recv.at[d])
        summed = shares[0].astype(f32)
        for w in range(1, NY):
            summed = summed + shares[w].astype(f32)
        return summed

    def up0_copy(w):
        return remote(
            push.at[0],
            first_in.at[side, :, own_span],
            up0_send.at[w],
            up0_recv.at[side, y],
            parent,
            w * NV + v,
        )

    def up_copy(k):
        return remote(
            push.at[k],
            later_in.at[side, k - 1],
            up_send.at[k],
            up_recv.at[side, k - 1],
            parent,
            y * NV + v,
        )

    def flat(k):
        return factor[k].reshape(span, width)

    def pushed(k, sample_half):
        return lax.dot_general(sample_half, flat(k), NT, preferred_element_type=f32)

    def cut_pieces(ref, value):
        parts = [value[:, 128 * a : 128 * (a + 1)] for a in range(span // 128)]
        for q in range(NV):
            a, b = divmod(q * rows, 128)
            moved = pltpu.roll(parts[a], 128 - b, axis=1) if b else parts[a]
            if b + rows > 128:
                after = pltpu.roll(parts[a + 1], 128 - b, axis=1)
                moved = jnp.where(lane < 128 - b, moved, after)
            ref[q] = moved.astype(ref.dtype)

    def sample_copy(d):
        to = (v + d) % NV
        return remote(
            piece_out.at[to], sample_in.at[v], sample_send.at[d], sample_recv.at[d], s, y * NV + to
        )

    def solved_copy(d):
        to = (v + d) % NV
        return remote(
            solved_out.at[to], solved_in.at[v], solved_send.at[d], solved_recv.at[d], s, y * NV + to
        )

    def last_copy(d):
        to = (c + d) % (NY * NV)
        return remote(
            last_out.at[to // NV, to % NV],
            last_in.at[c],
            last_send.at[d],
            last_recv.at[d],
            s,
            to,
        )

    def top_copy(i, d):
        to = (v + d) % NV
        ref, sem = (sample_in, sample_recv) if i == 0 else (solved_in, solved_recv)
        return remote(
            top_piece.at[i, to], ref.at[v], top_send.at[i, d], sem.at[d], root, y * NV + to
        )

    def sample_out():
        cut_pieces(piece_out, sample_t[:, own_span])
        sample_in[v] = piece_out[v]
        for d in range(1, NV):
            sample_copy(d).start()

    def move_inv():
        return remote(
            inv.at[y, x, core], top_inv.at[x, core], move_send.at[0], move_recv.at[0], top, c
        )

    def move_rhs():
        return remote(
            rhs_all.at[:, own_span], top_rhs, move_send.at[1], move_recv.at[1], top, c
        )

    def down_copy(k, child, i):
        return remote(
            above.at[k],
            above.at[k + 1],
            down_send.at[i, k],
            down_recv.at[k + 1],
            child,
            y * NV + v,
        )

    def down0_copy(w, child, i):
        return remote(
            part_out.at[w],
            parent_in.at[y],
            down0_send.at[i, w],
            down0_recv.at[y],
            child,
            w * NV + v,
        )

    def own_copy(d):
        to = (y + d) % NY
        return remote(part_out.at[to], own_in.at[y], own_send.at[d], own_recv.at[d], s, to * NV + v)

    def hand_down(k):
        @pl.when(has_kids)
        def _():
            down_copy(k, left, 0).start()
            down_copy(k, right, 1).start()

    def make_joint(k):
        for w in range(NY):
            start = w * span
            joint[k, :, start : start + span] = lax.dot_general(
                factor[k, :, :, :, start:].reshape(span, width - start),
                inv[w, :, :, :, start:].reshape(span, width - start),
                NT,
                preferred_element_type=f32,
            ).astype(bf16)

    def make_base():
        group = lax.broadcasted_iota(jnp.int32, (few, width), 1) // span
        total[...] = jnp.where(group == y, sample_t[...], 0.0)
        for k in range(slots - 1, 1, -1):

            @pl.when(level + k < slots)
            def _():
                arrived(above.at[k], down_recv.at[k])
                if k < slots - 1:
                    hand_down(k)
                total[...] -= jnp.dot(above[k], flat(k), preferred_element_type=f32)

        back = total[...].astype(bf16)
        for w in range(NY):
            start = w * span
            total[:, start : start + span] = lax.dot_general(
                back[:, start:],
                inv[w, :, :, :, start:].reshape(span, width - start),
                NT,
                preferred_element_type=f32,
            )

    @pl.when(is_leaf)
    def _():
        gx_start(0)
        for d in range(1, NV):
            rhs_copy(d).start()
        loads[2].wait()
        loads[3].wait()
        for k in range(slots):
            mask_slot(k)
        gx_pass(0, lambda j: gx_start(1) if j == 3 else None)
        join_rhs()
        gx_finish(0)
        share_start(rhs_all[:, own_span].astype(bf16), inv[y])
        gx_pass(1, lambda j: gx_start(2) if j == 3 and slots > 1 else None)
        sample_t[...] = share_sum()
        sample_half = sample_t[...].astype(bf16)
        for k in range(slots):
            if k > 0:
                gx_pass(
                    k + 1, lambda j: gx_start(k + 2) if j == 3 and k + 2 <= slots else None
                )
            gx_finish(k + 1)
            push[k] = pushed(k, sample_half).astype(bf16)
            if k == 0:
                for w in range(NY):
                    up0_copy(w).start()
            else:
                up_copy(k).start()
        for j in range(NX):
            gy_start(j)
        sample_out()
        gy_pass()
        gy_finish()
        make_joint(0)
        if slots > 1:
            make_joint(1)

    @pl.when(inner == 1)
    def _():
        @pl.when(is_root)
        def _():
            move_inv().start()

        @pl.when(not_root)
        def _():
            gx_start(0)
            gy_start(0)

        for d in range(1, NV):
            rhs_copy(d).start()
        loads[2].wait()
        loads[3].wait()
        for k in range(max(slots - 1, 1)):
            mask_slot(k)

        @pl.when(not_root)
        def _():
            def follow(j):
                gy_start(j)
                if j == 3:
                    gx_start(1)

            gx_pass(0, follow)

        join_rhs()

        @pl.when(is_root)
        def _():
            move_rhs().start()

        @pl.when(not_root)
        def _():
            for d in range(1, NY):
                row_copy(d).start()
            gx_pass(1)
            for k in range(1, slots - 1):

                @pl.when(level + k < slots)
                def _():
                    gx_start(k + 1)

            @pl.when(is_top)
            def _():
                arrived(top_inv.at[x, core], move_recv.at[0])
                gx_start(last)

            gy_pass()
            gx_finish(0)
            gx_finish(1)
            for d in range(1, NY):
                group_of = (y + NY - d) % NY
                arrived(
                    rhs_all.at[:, pl.ds(pl.multiple_of(group_of * span, 128), span)],
                    row_recv.at[d],
                )
            gy_finish()

            @pl.when(is_top)
            def _():
                gx_pass(last)
                gx_finish(last)
                arrived(top_rhs, move_recv.at[1])
                make_joint(0)

            for i in range(2):
                for w in range(NY):
                    arrived(first_in.at[i, :, w * span : (w + 1) * span], up0_recv.at[i, w])
            incoming = first_in[0].astype(f32) + first_in[1].astype(f32)
            residual = (rhs_all[...] - incoming).astype(bf16)
            for w in range(NY):
                to = (w + 1) * span
                sample_t[:, w * span : to] = jnp.dot(
                    residual[:, :to],
                    inv[: w + 1, :, :, :, w * span : to].reshape(to, span),
                    preferred_element_type=f32,
                )
            sample_half = sample_t[...].astype(bf16)

            def pushed_sum(k):
                out = pushed(k, sample_half)
                for i in range(2):
                    arrived(later_in.at[i, k], up_recv.at[i, k])
                return out + later_in[0, k].astype(f32) + later_in[1, k].astype(f32)

            @pl.when(has_parent)
            def _():
                push[0] = pushed_sum(0).astype(bf16)
                for w in range(NY):
                    up0_copy(w).start()

            @pl.when(is_top)
            def _():
                residual_root = (top_rhs[...] - pushed_sum(0)).astype(bf16)
                share_start(residual_root, top_inv[...])
                make_base()
                root_t = share_sum()
                root_sample[...] = root_t
                solved_root = lax.dot_general(
                    root_t.astype(bf16),
                    top_inv[...].reshape(span, width),
                    NT,
                    preferred_element_type=f32,
                )
                root_solved[...] = solved_root
                above[0] = solved_root.astype(bf16)
                down_copy(0, left, 0).start()
                down_copy(0, right, 1).start()

            for k in range(1, slots - 1):

                @pl.when(level + k < slots)
                def _():
                    gx_pass(k + 1)
                    gx_finish(k + 1)
                    push[k] = pushed_sum(k).astype(bf16)
                    up_copy(k).start()

            @pl.when(has_parent)
            def _():
                sample_out()
                make_joint(0)
                if slots > 1:
                    make_joint(1)

    @pl.when(not_root)
    def _():
        @pl.when(has_parent)
        def _():
            make_base()

            @pl.when(level + 1 < slots)
            def _():
                arrived(above.at[1], down_recv.at[1])
                hand_down(1)
                total[...] -= jnp.dot(above[1], joint[1], preferred_element_type=f32)

            for w in range(NY):
                arrived(parent_in.at[w], down0_recv.at[w])
            summed = parent_in[0].astype(f32)
            for w in range(1, NY):
                summed = summed + parent_in[w].astype(f32)
            above[0] = summed.astype(bf16)
            hand_down(0)

        for w in range(NY):
            lanes = slice(w * span, (w + 1) * span)
            part = total[:, lanes] - jnp.dot(
                above[0], joint[0, :, lanes], preferred_element_type=f32
            )
            part_out[w] = part.astype(bf16)

            @pl.when(is_leaf)
            def _():
                cut_pieces(last_out.at[w], part)

            @pl.when(has_kids)
            def _():
                down0_copy(w, left, 0).start()
                down0_copy(w, right, 1).start()

        @pl.when(is_leaf)
        def _():
            last_in[c] = last_out[y, v]
            for d in range(1, NY * NV):
                last_copy(d).start()

        @pl.when(has_kids)
        def _():
            own_in[y] = part_out[y]
            for d in ORDER:
                own_copy(d).start()

        @pl.when(is_top)
        def _():
            cut_pieces(top_piece.at[0], root_sample[:, own_span])
            cut_pieces(top_piece.at[1], root_solved[...])
            for d in range(NV):
                top_copy(0, d).start()
                top_copy(1, d).start()
            sample_out()

        for d in range(1, NV):
            arrived(sample_in.at[(v + NV - d) % NV], sample_recv.at[d])
        sample_ref[...] = sample_in[...].reshape(NV * few, 128).T[:rows, :]

        @pl.when(has_kids)
        def _():
            for d in ORDER:
                arrived(own_in.at[(y + NY - d) % NY], own_recv.at[d])
            solved = own_in[0].astype(f32)
            for w in range(1, NY):
                solved = solved + own_in[w].astype(f32)
            cut_pieces(solved_out, solved)
            solved_in[v] = solved_out[v]
            for d in range(1, NV):
                solved_copy(d).start()
            for d in range(1, NV):
                arrived(solved_in.at[(v + NV - d) % NV], solved_recv.at[d])
            answer_ref[...] = solved_in[...].reshape(NV * few, 128).T[:rows, :]

        @pl.when(is_leaf)
        def _():
            for d in range(1, NY * NV):
                source = (c + NY * NV - d) % (NY * NV)
                arrived(last_in.at[source], last_recv.at[d])
            pieces = last_in[0:NV].astype(f32)
            for w in range(1, NY):
                pieces = pieces + last_in[w * NV : (w + 1) * NV].astype(f32)
            answer_ref[...] = pieces.reshape(NV * few, 128).T[:rows, :]

    @pl.when(is_root)
    def _():
        for d in range(NV):
            arrived(sample_in.at[(v + NV - d) % NV], sample_recv.at[d])
            arrived(solved_in.at[(v + NV - d) % NV], solved_recv.at[d])
        sample_ref[...] = sample_in[...].reshape(NV * few, 128).T[:rows, :]
        answer_ref[...] = solved_in[...].reshape(NV * few, 128).T[:rows, :]

    for d in range(1, NV):
        rhs_copy(d).wait_send()

    def gx_sent(g):
        for i in range(2 * NX - 1):
            gx_copy(g, i).wait_send()

    @pl.when(is_root)
    def _():
        move_inv().wait_send()
        move_rhs().wait_send()

    @pl.when(not_root)
    def _():
        gx_sent(0)
        for k in range(slots):

            @pl.when(level + k < slots)
            def _():
                gx_sent(k + 1)

        def gy_sent(yy):
            for d in ORDER:
                for j in range(NX):
                    gy_copy(yy, d, j).wait_send()
                gs_copy(yy, d).wait_send()

        each_y(gy_sent)
        for d in range(1, NV):
            sample_copy(d).wait_send()

    @pl.when(has_kids)
    def _():
        for d in range(1, NV):
            solved_copy(d).wait_send()
        for d in ORDER:
            own_copy(d).wait_send()
        for d in range(1, NY):
            row_copy(d).wait_send()
        for i, child in enumerate((left, right)):
            for w in range(NY):
                down0_copy(w, child, i).wait_send()
            for k in range(slots - 1):

                @pl.when(level + k < slots)
                def _():
                    down_copy(k, child, i).wait_send()

    @pl.when(has_parent)
    def _():
        for w in range(NY):
            up0_copy(w).wait_send()
        for k in range(1, slots):

            @pl.when(level + k < slots)
            def _():
                up_copy(k).wait_send()

    def share_sent():
        for d in ORDER:
            share_copy(d).wait_send()

    @pl.when(is_leaf)
    def _():
        share_sent()
        for d in range(1, NY * NV):
            last_copy(d).wait_send()

    @pl.when(is_top)
    def _():
        share_sent()
        gx_sent(last)
        for d in range(NV):
            top_copy(0, d).wait_send()
            top_copy(1, d).wait_send()


def on_device(nodes, rhs, panel, inverse_t, pattern):
    rows, count = rhs.shape[1:]
    slots = panel.shape[1]
    width = inverse_t.shape[2]
    span = NV * rows
    few = count // NV
    f32, bf16 = jnp.float32, jnp.bfloat16
    dma = pltpu.SemaphoreType.DMA
    vmem = pl.BlockSpec(memory_space=pltpu.VMEM)
    outs = pl.pallas_call(
        functools.partial(kernel, nodes),
        out_shape=[jax.ShapeDtypeStruct((rows, count), f32)] * 2,
        in_specs=[pl.BlockSpec(memory_space=pltpu.HBM)] * 4,
        out_specs=[vmem, vmem],
        scratch_shapes=[
            pltpu.VMEM((rows, count), f32),
            pltpu.VMEM((slots, rows, width), bf16),
            pltpu.SMEM(pattern.shape[1:], jnp.int32),
            pltpu.VMEM((slots, NX, 2, rows, width), bf16),
            pltpu.VMEM((NY, NX, 2, rows, width), bf16),
            pltpu.VMEM((NX, 2, rows, width), bf16),
            pltpu.VMEM((NV, few, 128), f32),
            pltpu.VMEM((NV, few, 128), f32),
            pltpu.VMEM((few, width), f32),
            pltpu.VMEM((few, span), f32),
            pltpu.VMEM((2, few, width), bf16),
            pltpu.VMEM((2, max(slots - 1, 1), few, span), bf16),
            pltpu.VMEM((slots, few, span), bf16),
            pltpu.VMEM((NY, few, width), bf16),
            pltpu.VMEM((few, width), f32),
            pltpu.VMEM((few, width), f32),
            pltpu.VMEM((NV, few, 128), f32),
            pltpu.VMEM((NV, few, 128), f32),
            pltpu.VMEM((NY, few, span), bf16),
            pltpu.VMEM((slots, few, span), bf16),
            pltpu.VMEM((NY, few, span), bf16),
            pltpu.VMEM((NY, few, span), bf16),
            pltpu.VMEM((NV, few, 128), f32),
            pltpu.VMEM((NV, few, 128), f32),
            pltpu.VMEM((2, NV, few, 128), f32),
            pltpu.VMEM((few, width), f32),
            pltpu.VMEM((few, span), f32),
        ]
        + [dma((slots + 2, 2 * NX - 1))] * 2
        + [dma((NY, NX))] * 2
        + [dma((NY,))] * 2
        + [dma((NV,))] * 2
        + [dma((NY,))] * 2
        + [dma((NY,))] * 2
        + [dma((NY,)), dma((2, NY))]
        + [dma((slots,)), dma((2, slots))]
        + [dma((2, NY)), dma((NY,))]
        + [dma((2, slots)), dma((slots,))]
        + [dma((NY,))] * 2
        + [dma((NV,))] * 4
        + [dma((2,))] * 2
        + [dma((2, NV))]
        + [dma((4,)), pltpu.VMEM((2, span, width), bf16)]
        + [pltpu.VMEM((NY, NV, few, 128), bf16), pltpu.VMEM((NY * NV, few, 128), bf16)]
        + [dma((NY * NV,))] * 2,
        compiler_params=pltpu.CompilerParams(
            collective_id=0, has_side_effects=True, vmem_limit_bytes=56 * 2**20
        ),
    )(rhs[0], panel[0], inverse_t[0], pattern[0])
    return outs[0][None], outs[1][None]


def solution(mesh):
    in_specs = (
        P("lvl", "col", None),
        P("lvl", None, "col", None),
        P("lvl", "col", None),
        P("lvl", None, None, None),
    )
    out_specs = (P("lvl", "col", None), P("lvl", "col", None))
    return jax.shard_map(
        functools.partial(on_device, mesh.shape["lvl"]),
        mesh=mesh,
        in_specs=in_specs,
        out_specs=out_specs,
        check_vma=False,
    )
```

```python
import functools

import jax
import jax.numpy as jnp
from jax import lax
from jax.experimental import pallas as pl
from jax.experimental.pallas import tpu as pltpu
from jax.sharding import PartitionSpec as P

MESH = pl.DeviceIdType.MESH
NT = (((1,), (1,)), ((), ()))
NX = 4
NY = 4
NV = 2 * NX
ORDER = (1, 3, 2)


def remote(src, dst, send_sem, recv_sem, lvl, col):
    return pltpu.make_async_remote_copy(
        src_ref=src,
        dst_ref=dst,
        send_sem=send_sem,
        recv_sem=recv_sem,
        device_id=(lvl, col),
        device_id_type=MESH,
    )


def arrived(dst, sem):
    pltpu.make_async_copy(dst, dst, sem).wait()


def kernel(
    nodes,
    rhs_ref,
    panel_ref,
    inverse_ref,
    pattern_ref,
    sample_ref,
    answer_ref,
    rhs_own,
    panel_own,
    pattern_own,
    factor,
    inv,
    top_inv,
    turned,
    rhs_in,
    rhs_all,
    top_rhs,
    first_in,
    later_in,
    push,
    shares,
    sample_t,
    total,
    piece_out,
    sample_in,
    parent_in,
    above,
    part_out,
    own_in,
    solved_out,
    solved_in,
    top_piece,
    root_sample,
    root_solved,
    gx_send,
    gx_recv,
    gy_send,
    gy_recv,
    gs_send,
    gs_recv,
    rhs_send,
    rhs_recv,
    row_send,
    row_recv,
    share_send,
    share_recv,
    up0_send,
    up0_recv,
    up_send,
    up_recv,
    down0_send,
    down0_recv,
    down_send,
    down_recv,
    own_send,
    own_recv,
    sample_send,
    sample_recv,
    solved_send,
    solved_recv,
    move_send,
    move_recv,
    top_send,
    load_sem,
    joint,
    last_out,
    last_in,
    last_send,
    last_recv,
):
    rows = rhs_ref.shape[0]
    width = inv.shape[-1]
    slots = panel_ref.shape[0]
    tiles = pattern_ref.shape[2]
    tile = width // tiles
    span = NV * rows
    few = rhs_ref.shape[1] // NV
    f32, bf16 = jnp.float32, jnp.bfloat16
    root, top = nodes - 1, nodes // 2 - 1

    s = lax.axis_index("lvl")
    c = lax.axis_index("col")
    y, v = c // NV, c % NV
    x, core = v // 2, v % 2
    other = 1 - core

    level = 0
    step = 1
    for e in range(1, slots + 1):
        whole = 1 - ((s + 1) % 2**e + 2**e - 1) // 2**e
        level = level + whole
        step = step + whole * 2 ** (e - 1)
    side = (s // (2 * step)) % 2
    parent = (s + step * (1 - 2 * side)) % nodes
    above_at = [parent]
    for k in range(1, slots):
        far = step * 2**k
        above_at.append(
            (above_at[-1] + far * (1 - 2 * ((above_at[-1] // (2 * far)) % 2)) + nodes) % nodes
        )
    left = (s + nodes - step // 2) % nodes
    right = (s + step // 2) % nodes
    one_root = (s + 1) // nodes
    one_top = (level + 1) // slots - one_root
    inner = s % 2
    is_root = one_root == 1
    is_top = one_top == 1
    not_root = one_root == 0
    is_leaf = inner == 0
    has_kids = inner * (1 - one_root) == 1
    has_parent = one_root + one_top == 0

    def chip(yy, xx, cc):
        return (yy * NX + xx) * 2 + cc

    own_span = pl.ds(pl.multiple_of(y * span, 128), span)

    barrier = pltpu.get_barrier_semaphore()

    def greet(lvl, col):
        pl.semaphore_signal(barrier, inc=1, device_id=(lvl, col), device_id_type=MESH)

    @pl.when(is_leaf)
    def _():
        for d in range(1, NY * NV):
            greet(s, (c + d) % (NY * NV))

    @pl.when(inner == 1)
    def _():
        for d in range(1, NV):
            greet(s, y * NV + (v + d) % NV)
        for d in range(1, NY):
            greet(s, (y + d) % NY * NV + v)

    @pl.when(has_parent)
    def _():
        for w in range(NY):
            greet(parent, w * NV + v)

    @pl.when(has_kids)
    def _():
        for w in range(NY):
            greet(left, w * NV + v)
            greet(right, w * NV + v)

    @pl.when(is_top)
    def _():
        for q in range(NV):
            greet(root, y * NV + q)

    @pl.when(is_root)
    def _():
        for q in range(NV):
            greet(top, y * NV + q)

    def below(t):
        return [i for i in range(2 ** (t + 1) - 1) if i != 2**t - 1]

    for t in range(2, slots):

        @pl.when(level == t)
        def _(t=t):
            for i in below(t):
                if (i + 1) % 2 ** (t - 1):
                    greet((s + nodes - 2**t + 1 + i) % nodes, c)

    far_count = 0
    for k in range(2, slots):
        far_count = far_count + (slots - 1 - level + slots - k) // slots

    loads = (
        pltpu.make_async_copy(rhs_ref, rhs_own, load_sem.at[0]),
        pltpu.make_async_copy(inverse_ref, inv.at[y, x, core], load_sem.at[1]),
        pltpu.make_async_copy(pattern_ref, pattern_own, load_sem.at[2]),
        pltpu.make_async_copy(panel_ref, panel_own, load_sem.at[3]),
    )
    for load in loads:
        load.start()
    piece = 16

    def mask_slot(k):
        for q in range(rows // piece):
            tile_row = (c * rows + q * piece) // tile
            for j in range(tiles):
                keep = pattern_own[k, tile_row, j].astype(f32)
                part = (slice(q * piece, (q + 1) * piece), slice(j * tile, (j + 1) * tile))
                block = panel_own[(k,) + part]
                factor[(k, x, core) + part] = (block.astype(f32) * keep).astype(bf16)

    loads[0].wait()
    padded = jnp.concatenate(
        [rhs_own[...], jnp.zeros((128 - rows, rhs_ref.shape[1]), f32)], axis=0
    )
    turned[...] = padded.T.reshape(NV, few, 128)
    rhs_in[v] = turned[v]
    loads[1].wait()

    pl.semaphore_wait(
        barrier,
        (NV - 1 + NY - 1) * inner
        + (NV * NY - 1) * (1 - inner)
        + NY * (1 - one_root - one_top)
        + 2 * NY * inner * (1 - one_root)
        + NV * (one_top + one_root)
        + far_count,
    )

    last = slots + 1

    def block(g, xx, cc):
        if g == 0:
            return inv.at[y, xx, cc]
        if g == last:
            return top_inv.at[xx, cc]
        return factor.at[g - 1, xx, cc]

    def gx_copy(g, i):
        if i == 0:
            ref, col = block(g, x, core), chip(y, x, other)
        elif i < NX:
            ref, col = block(g, x, core), chip(y, (x + i) % NX, core)
        else:
            ref, col = block(g, (x + 2 * NX - 1 - i) % NX, core), chip(y, x, other)
        return remote(ref, ref, gx_send.at[g, i], gx_recv.at[g, i], s, col)

    def gx_wait(g, i):
        if i == 0:
            ref = block(g, x, other)
        elif i < NX:
            ref = block(g, (x + NX - i) % NX, core)
        else:
            ref = block(g, (x + 2 * NX - 1 - i) % NX, other)
        arrived(ref, gx_recv.at[g, i])

    def gx_start(g):
        for i in ORDER + (0,):
            gx_copy(g, i).start()

    def gx_pass(g, then=None):
        for i in ORDER:
            gx_wait(g, i)
            gx_copy(g, i + NX - 1).start()
            if then is not None:
                then(NX - i)

    def gx_finish(g):
        for i in (0,) + tuple(i + NX - 1 for i in ORDER):
            gx_wait(g, i)

    def each_y(body):
        for yy in range(NY):

            @pl.when(y == yy)
            def _(yy=yy):
                body(yy)

    def gy_copy(yy, d, j):
        ref = inv.at[yy, (x + j) % NX, core, :, yy * span :]
        col = chip((yy + d) % NY, x, core)
        return remote(ref, ref, gy_send.at[d, j], gy_recv.at[d, j], s, col)

    def gs_copy(yy, d):
        source = (yy + NY - d) % NY
        ref = inv.at[source, :, core, :, source * span :]
        return remote(ref, ref, gs_send.at[d], gs_recv.at[d], s, chip(yy, x, other))

    def gy_start(j):
        def body(yy):
            for d in ORDER:
                gy_copy(yy, d, j).start()

        each_y(body)

    def gy_pass():
        def body(yy):
            for d in ORDER:
                source = (yy + NY - d) % NY
                for j in range(NX):
                    arrived(
                        inv.at[source, (x + j) % NX, core, :, source * span :], gy_recv.at[d, j]
                    )
                gs_copy(yy, d).start()

        each_y(body)

    def gy_finish():
        def body(yy):
            for d in ORDER:
                source = (yy + NY - d) % NY
                arrived(inv.at[source, :, other, :, source * span :], gs_recv.at[d])

        each_y(body)

    def rhs_copy(d):
        to = (v + d) % NV
        return remote(turned.at[to], rhs_in.at[v], rhs_send.at[d], rhs_recv.at[d], s, y * NV + to)

    def row_copy(d):
        ref = rhs_all.at[:, own_span]
        return remote(ref, ref, row_send.at[d], row_recv.at[d], s, (y + d) % NY * NV + v)

    lane = lax.broadcasted_iota(jnp.int32, (few, 128), 1)

    def join_rhs():
        for d in range(1, NV):
            arrived(rhs_in.at[(v + NV - d) % NV], rhs_recv.at[d])
        joined = [jnp.zeros((few, 128), f32) for _ in range(span // 128)]
        for q in range(NV):
            a, b = divmod(q * rows, 128)
            moved = pltpu.roll(rhs_in[q], b, axis=1) if b else rhs_in[q]
            if b + rows <= 128:
                joined[a] = joined[a] + moved
            else:
                joined[a] = joined[a] + jnp.where(lane >= b, moved, 0.0)
                joined[a + 1] = joined[a + 1] + jnp.where(lane >= b, 0.0, moved)
        rhs_all[:, own_span] = jnp.concatenate(joined, axis=1)

    def share_copy(d):
        ref = shares.at[y]
        return remote(ref, ref, share_send.at[d], share_recv.at[d], s, (y + d) % NY * NV + v)

    def share_start(residual, rows_of):
        product = jnp.dot(residual, rows_of.reshape(span, width), preferred_element_type=f32)
        shares[y] = product.astype(bf16)
        for d in ORDER:
            share_copy(d).start()

    def share_sum():
        for d in ORDER:
            arrived(shares.at[(y + NY - d) % NY], share_recv.at[d])
        summed = shares[0].astype(f32)
        for w in range(1, NY):
            summed = summed + shares[w].astype(f32)
        return summed

    def up0_copy(w):
        return remote(
            push.at[0],
            first_in.at[side, :, own_span],
            up0_send.at[w],
            up0_recv.at[side, y],
            parent,
            w * NV + v,
        )

    def up_copy(k):
        return remote(
            push.at[k],
            later_in.at[s % (step * 2 ** (k + 1))],
            up_send.at[k],
            up_recv.at[s % (step * 2 ** (k + 1))],
            above_at[k - 1],
            y * NV + v,
        )

    def flat(k):
        return factor[k].reshape(span, width)

    def pushed(k, sample_half):
        return lax.dot_general(sample_half, flat(k), NT, preferred_element_type=f32)

    def cut_pieces(ref, value):
        parts = [value[:, 128 * a : 128 * (a + 1)] for a in range(span // 128)]
        for q in range(NV):
            a, b = divmod(q * rows, 128)
            moved = pltpu.roll(parts[a], 128 - b, axis=1) if b else parts[a]
            if b + rows > 128:
                after = pltpu.roll(parts[a + 1], 128 - b, axis=1)
                moved = jnp.where(lane < 128 - b, moved, after)
            ref[q] = moved.astype(ref.dtype)

    def sample_copy(d):
        to = (v + d) % NV
        return remote(
            piece_out.at[to], sample_in.at[v], sample_send.at[d], sample_recv.at[d], s, y * NV + to
        )

    def solved_copy(d):
        to = (v + d) % NV
        return remote(
            solved_out.at[to], solved_in.at[v], solved_send.at[d], solved_recv.at[d], s, y * NV + to
        )

    def last_copy(d):
        to = (c + d) % (NY * NV)
        return remote(
            last_out.at[to // NV, to % NV],
            last_in.at[c],
            last_send.at[d],
            last_recv.at[d],
            s,
            to,
        )

    def top_copy(i, d):
        to = (v + d) % NV
        ref, sem = (sample_in, sample_recv) if i == 0 else (solved_in, solved_recv)
        return remote(
            top_piece.at[i, to], ref.at[v], top_send.at[i, d], sem.at[d], root, y * NV + to
        )

    def sample_out():
        cut_pieces(piece_out, sample_t[:, own_span])
        sample_in[v] = piece_out[v]
        for d in range(1, NV):
            sample_copy(d).start()

    def move_inv():
        return remote(
            inv.at[y, x, core], top_inv.at[x, core], move_send.at[0], move_recv.at[0], top, c
        )

    def move_rhs():
        return remote(
            rhs_all.at[:, own_span], top_rhs, move_send.at[1], move_recv.at[1], top, c
        )

    def down_copy(k, child, i):
        return remote(
            above.at[k],
            above.at[k + 1],
            down_send.at[i, k],
            down_recv.at[k + 1],
            child,
            y * NV + v,
        )

    def down0_copy(w, child, i):
        return remote(
            part_out.at[w],
            parent_in.at[y],
            down0_send.at[i, w],
            down0_recv.at[y],
            child,
            w * NV + v,
        )

    def own_copy(d):
        to = (y + d) % NY
        return remote(part_out.at[to], own_in.at[y], own_send.at[d], own_recv.at[d], s, to * NV + v)

    def hand_down(k):
        @pl.when(has_kids)
        def _():
            down_copy(k, left, 0).start()
            down_copy(k, right, 1).start()

    def make_joint(k):
        for w in range(NY):
            start = w * span
            joint[k, :, start : start + span] = lax.dot_general(
                factor[k, :, :, :, start:].reshape(span, width - start),
                inv[w, :, :, :, start:].reshape(span, width - start),
                NT,
                preferred_element_type=f32,
            ).astype(bf16)

    def make_base():
        group = lax.broadcasted_iota(jnp.int32, (few, width), 1) // span
        total[...] = jnp.where(group == y, sample_t[...], 0.0)
        for k in range(slots - 1, 1, -1):

            @pl.when(level + k < slots)
            def _():
                arrived(above.at[k], down_recv.at[k])
                if k < slots - 1:
                    hand_down(k)
                total[...] -= jnp.dot(above[k], flat(k), preferred_element_type=f32)

        back = total[...].astype(bf16)
        for w in range(NY):
            start = w * span
            total[:, start : start + span] = lax.dot_general(
                back[:, start:],
                inv[w, :, :, :, start:].reshape(span, width - start),
                NT,
                preferred_element_type=f32,
            )

    @pl.when(is_leaf)
    def _():
        gx_start(0)
        for d in range(1, NV):
            rhs_copy(d).start()
        loads[2].wait()
        loads[3].wait()
        for k in range(slots):
            mask_slot(k)
        gx_pass(0, lambda j: gx_start(1) if j == 3 else None)
        join_rhs()
        gx_finish(0)
        share_start(rhs_all[:, own_span].astype(bf16), inv[y])
        gx_pass(1, lambda j: gx_start(2) if j == 3 and slots > 1 else None)
        sample_t[...] = share_sum()
        sample_half = sample_t[...].astype(bf16)
        for k in range(slots):
            if k > 0:
                gx_pass(
                    k + 1, lambda j: gx_start(k + 2) if j == 3 and k + 2 <= slots else None
                )
            gx_finish(k + 1)
            push[k] = pushed(k, sample_half).astype(bf16)
            if k == 0:
                for w in range(NY):
                    up0_copy(w).start()
            else:
                up_copy(k).start()
        for j in range(NX):
            gy_start(j)
        sample_out()
        gy_pass()
        gy_finish()
        make_joint(0)
        if slots > 1:
            make_joint(1)

    @pl.when(inner == 1)
    def _():
        @pl.when(is_root)
        def _():
            move_inv().start()

        @pl.when(not_root)
        def _():
            gx_start(0)
            gy_start(0)

        for d in range(1, NV):
            rhs_copy(d).start()
        loads[2].wait()
        loads[3].wait()
        for k in range(max(slots - 1, 1)):
            mask_slot(k)

        @pl.when(not_root)
        def _():
            def follow(j):
                gy_start(j)
                if j == 3:
                    gx_start(1)

            gx_pass(0, follow)

        join_rhs()

        @pl.when(is_root)
        def _():
            move_rhs().start()

        @pl.when(not_root)
        def _():
            for d in range(1, NY):
                row_copy(d).start()
            gx_pass(1)
            for k in range(1, slots - 1):

                @pl.when(level + k < slots)
                def _():
                    gx_start(k + 1)

            @pl.when(is_top)
            def _():
                arrived(top_inv.at[x, core], move_recv.at[0])
                gx_start(last)

            gy_pass()
            gx_finish(0)
            gx_finish(1)
            for d in range(1, NY):
                group_of = (y + NY - d) % NY
                arrived(
                    rhs_all.at[:, pl.ds(pl.multiple_of(group_of * span, 128), span)],
                    row_recv.at[d],
                )
            gy_finish()

            @pl.when(is_top)
            def _():
                gx_pass(last)
                gx_finish(last)
                arrived(top_rhs, move_recv.at[1])
                make_joint(0)

            for i in range(2):
                for w in range(NY):
                    arrived(first_in.at[i, :, w * span : (w + 1) * span], up0_recv.at[i, w])
            incoming = first_in[0].astype(f32) + first_in[1].astype(f32)
            residual = (rhs_all[...] - incoming).astype(bf16)
            for w in range(NY):
                to = (w + 1) * span
                sample_t[:, w * span : to] = jnp.dot(
                    residual[:, :to],
                    inv[: w + 1, :, :, :, w * span : to].reshape(to, span),
                    preferred_element_type=f32,
                )
            sample_half = sample_t[...].astype(bf16)

            def pushed_sum(t):
                out = pushed(0, sample_half)
                for i in below(t):
                    arrived(later_in.at[i], up_recv.at[i])
                    out = out + later_in[i].astype(f32)
                return out

            for t in range(1, slots - 1):

                @pl.when(level == t)
                def _(t=t):
                    push[0] = pushed_sum(t).astype(bf16)
                    for w in range(NY):
                        up0_copy(w).start()

            @pl.when(is_top)
            def _():
                residual_root = (top_rhs[...] - pushed_sum(slots - 1)).astype(bf16)
                share_start(residual_root, top_inv[...])
                make_base()
                root_t = share_sum()
                root_sample[...] = root_t
                solved_root = lax.dot_general(
                    root_t.astype(bf16),
                    top_inv[...].reshape(span, width),
                    NT,
                    preferred_element_type=f32,
                )
                root_solved[...] = solved_root
                above[0] = solved_root.astype(bf16)
                down_copy(0, left, 0).start()
                down_copy(0, right, 1).start()

            for k in range(1, slots - 1):

                @pl.when(level + k < slots)
                def _():
                    gx_pass(k + 1)
                    gx_finish(k + 1)
                    push[k] = pushed(k, sample_half).astype(bf16)
                    up_copy(k).start()

            @pl.when(has_parent)
            def _():
                sample_out()
                make_joint(0)
                if slots > 1:
                    make_joint(1)

    @pl.when(not_root)
    def _():
        @pl.when(has_parent)
        def _():
            make_base()

            @pl.when(level + 1 < slots)
            def _():
                arrived(above.at[1], down_recv.at[1])
                hand_down(1)
                total[...] -= jnp.dot(above[1], joint[1], preferred_element_type=f32)

            for w in range(NY):
                arrived(parent_in.at[w], down0_recv.at[w])
            summed = parent_in[0].astype(f32)
            for w in range(1, NY):
                summed = summed + parent_in[w].astype(f32)
            above[0] = summed.astype(bf16)
            hand_down(0)

        for w in range(NY):
            lanes = slice(w * span, (w + 1) * span)
            part = total[:, lanes] - jnp.dot(
                above[0], joint[0, :, lanes], preferred_element_type=f32
            )
            part_out[w] = part.astype(bf16)

            @pl.when(is_leaf)
            def _():
                cut_pieces(last_out.at[w], part)

            @pl.when(has_kids)
            def _():
                down0_copy(w, left, 0).start()
                down0_copy(w, right, 1).start()

        @pl.when(is_leaf)
        def _():
            last_in[c] = last_out[y, v]
            for d in range(1, NY * NV):
                last_copy(d).start()

        @pl.when(has_kids)
        def _():
            own_in[y] = part_out[y]
            for d in ORDER:
                own_copy(d).start()

        @pl.when(is_top)
        def _():
            cut_pieces(top_piece.at[0], root_sample[:, own_span])
            cut_pieces(top_piece.at[1], root_solved[...])
            for d in range(NV):
                top_copy(0, d).start()
                top_copy(1, d).start()
            sample_out()

        for d in range(1, NV):
            arrived(sample_in.at[(v + NV - d) % NV], sample_recv.at[d])
        sample_ref[...] = sample_in[...].reshape(NV * few, 128).T[:rows, :]

        @pl.when(has_kids)
        def _():
            for d in ORDER:
                arrived(own_in.at[(y + NY - d) % NY], own_recv.at[d])
            solved = own_in[0].astype(f32)
            for w in range(1, NY):
                solved = solved + own_in[w].astype(f32)
            cut_pieces(solved_out, solved)
            solved_in[v] = solved_out[v]
            for d in range(1, NV):
                solved_copy(d).start()
            for d in range(1, NV):
                arrived(solved_in.at[(v + NV - d) % NV], solved_recv.at[d])
            answer_ref[...] = solved_in[...].reshape(NV * few, 128).T[:rows, :]

        @pl.when(is_leaf)
        def _():
            for d in range(1, NY * NV):
                source = (c + NY * NV - d) % (NY * NV)
                arrived(last_in.at[source], last_recv.at[d])
            pieces = last_in[0:NV].astype(f32)
            for w in range(1, NY):
                pieces = pieces + last_in[w * NV : (w + 1) * NV].astype(f32)
            answer_ref[...] = pieces.reshape(NV * few, 128).T[:rows, :]

    @pl.when(is_root)
    def _():
        for d in range(NV):
            arrived(sample_in.at[(v + NV - d) % NV], sample_recv.at[d])
            arrived(solved_in.at[(v + NV - d) % NV], solved_recv.at[d])
        sample_ref[...] = sample_in[...].reshape(NV * few, 128).T[:rows, :]
        answer_ref[...] = solved_in[...].reshape(NV * few, 128).T[:rows, :]

    for d in range(1, NV):
        rhs_copy(d).wait_send()

    def gx_sent(g):
        for i in range(2 * NX - 1):
            gx_copy(g, i).wait_send()

    @pl.when(is_root)
    def _():
        move_inv().wait_send()
        move_rhs().wait_send()

    @pl.when(not_root)
    def _():
        gx_sent(0)
        for k in range(slots):

            @pl.when(level + k < slots)
            def _():
                gx_sent(k + 1)

        def gy_sent(yy):
            for d in ORDER:
                for j in range(NX):
                    gy_copy(yy, d, j).wait_send()
                gs_copy(yy, d).wait_send()

        each_y(gy_sent)
        for d in range(1, NV):
            sample_copy(d).wait_send()

    @pl.when(has_kids)
    def _():
        for d in range(1, NV):
            solved_copy(d).wait_send()
        for d in ORDER:
            own_copy(d).wait_send()
        for d in range(1, NY):
            row_copy(d).wait_send()
        for i, child in enumerate((left, right)):
            for w in range(NY):
                down0_copy(w, child, i).wait_send()
            for k in range(slots - 1):

                @pl.when(level + k < slots)
                def _():
                    down_copy(k, child, i).wait_send()

    @pl.when(has_parent)
    def _():
        for w in range(NY):
            up0_copy(w).wait_send()
        for k in range(1, slots):

            @pl.when(level + k < slots)
            def _():
                up_copy(k).wait_send()

    def share_sent():
        for d in ORDER:
            share_copy(d).wait_send()

    @pl.when(is_leaf)
    def _():
        share_sent()
        for d in range(1, NY * NV):
            last_copy(d).wait_send()

    @pl.when(is_top)
    def _():
        share_sent()
        gx_sent(last)
        for d in range(NV):
            top_copy(0, d).wait_send()
            top_copy(1, d).wait_send()


def on_device(nodes, rhs, panel, inverse_t, pattern):
    rows, count = rhs.shape[1:]
    slots = panel.shape[1]
    width = inverse_t.shape[2]
    span = NV * rows
    few = count // NV
    f32, bf16 = jnp.float32, jnp.bfloat16
    dma = pltpu.SemaphoreType.DMA
    vmem = pl.BlockSpec(memory_space=pltpu.VMEM)
    outs = pl.pallas_call(
        functools.partial(kernel, nodes),
        out_shape=[jax.ShapeDtypeStruct((rows, count), f32)] * 2,
        in_specs=[pl.BlockSpec(memory_space=pltpu.HBM)] * 4,
        out_specs=[vmem, vmem],
        scratch_shapes=[
            pltpu.VMEM((rows, count), f32),
            pltpu.VMEM((slots, rows, width), bf16),
            pltpu.SMEM(pattern.shape[1:], jnp.int32),
            pltpu.VMEM((slots, NX, 2, rows, width), bf16),
            pltpu.VMEM((NY, NX, 2, rows, width), bf16),
            pltpu.VMEM((NX, 2, rows, width), bf16),
            pltpu.VMEM((NV, few, 128), f32),
            pltpu.VMEM((NV, few, 128), f32),
            pltpu.VMEM((few, width), f32),
            pltpu.VMEM((few, span), f32),
            pltpu.VMEM((2, few, width), bf16),
            pltpu.VMEM((2**slots - 1, few, span), bf16),
            pltpu.VMEM((slots, few, span), bf16),
            pltpu.VMEM((NY, few, width), bf16),
            pltpu.VMEM((few, width), f32),
            pltpu.VMEM((few, width), f32),
            pltpu.VMEM((NV, few, 128), f32),
            pltpu.VMEM((NV, few, 128), f32),
            pltpu.VMEM((NY, few, span), bf16),
            pltpu.VMEM((slots, few, span), bf16),
            pltpu.VMEM((NY, few, span), bf16),
            pltpu.VMEM((NY, few, span), bf16),
            pltpu.VMEM((NV, few, 128), f32),
            pltpu.VMEM((NV, few, 128), f32),
            pltpu.VMEM((2, NV, few, 128), f32),
            pltpu.VMEM((few, width), f32),
            pltpu.VMEM((few, span), f32),
        ]
        + [dma((slots + 2, 2 * NX - 1))] * 2
        + [dma((NY, NX))] * 2
        + [dma((NY,))] * 2
        + [dma((NV,))] * 2
        + [dma((NY,))] * 2
        + [dma((NY,))] * 2
        + [dma((NY,)), dma((2, NY))]
        + [dma((slots,)), dma((2**slots - 1,))]
        + [dma((2, NY)), dma((NY,))]
        + [dma((2, slots)), dma((slots,))]
        + [dma((NY,))] * 2
        + [dma((NV,))] * 4
        + [dma((2,))] * 2
        + [dma((2, NV))]
        + [dma((4,)), pltpu.VMEM((2, span, width), bf16)]
        + [pltpu.VMEM((NY, NV, few, 128), bf16), pltpu.VMEM((NY * NV, few, 128), bf16)]
        + [dma((NY * NV,))] * 2,
        compiler_params=pltpu.CompilerParams(
            collective_id=0, has_side_effects=True, vmem_limit_bytes=56 * 2**20
        ),
    )(rhs[0], panel[0], inverse_t[0], pattern[0])
    return outs[0][None], outs[1][None]


def solution(mesh):
    in_specs = (
        P("lvl", "col", None),
        P("lvl", None, "col", None),
        P("lvl", "col", None),
        P("lvl", None, None, None),
    )
    out_specs = (P("lvl", "col", None), P("lvl", "col", None))
    return jax.shard_map(
        functools.partial(on_device, mesh.shape["lvl"]),
        mesh=mesh,
        in_specs=in_specs,
        out_specs=out_specs,
        check_vma=False,
    )
```

```python
import functools

import jax
import jax.numpy as jnp
from jax import lax
from jax.experimental import pallas as pl
from jax.experimental.pallas import tpu as pltpu
from jax.sharding import PartitionSpec as P

MESH = pl.DeviceIdType.MESH
NT = (((1,), (1,)), ((), ()))
NX = 4
NY = 4
NV = 2 * NX
ORDER = (1, 3, 2)


def remote(src, dst, send_sem, recv_sem, lvl, col):
    return pltpu.make_async_remote_copy(
        src_ref=src,
        dst_ref=dst,
        send_sem=send_sem,
        recv_sem=recv_sem,
        device_id=(lvl, col),
        device_id_type=MESH,
    )


def arrived(dst, sem):
    pltpu.make_async_copy(dst, dst, sem).wait()


def kernel(
    nodes,
    rhs_ref,
    panel_ref,
    inverse_ref,
    pattern_ref,
    sample_ref,
    answer_ref,
    rhs_own,
    panel_own,
    pattern_own,
    factor,
    inv,
    top_inv,
    turned,
    rhs_in,
    rhs_all,
    top_rhs,
    first_in,
    later_in,
    push,
    shares,
    sample_t,
    total,
    piece_out,
    sample_in,
    parent_in,
    above,
    part_out,
    own_in,
    solved_out,
    solved_in,
    top_piece,
    root_sample,
    root_solved,
    gx_send,
    gx_recv,
    gy_send,
    gy_recv,
    gs_send,
    gs_recv,
    rhs_send,
    rhs_recv,
    row_send,
    row_recv,
    share_send,
    share_recv,
    up0_send,
    up0_recv,
    up_send,
    up_recv,
    down0_send,
    down0_recv,
    down_send,
    down_recv,
    own_send,
    own_recv,
    sample_send,
    sample_recv,
    solved_send,
    solved_recv,
    move_send,
    move_recv,
    top_send,
    load_sem,
    joint,
    last_out,
    last_in,
    last_send,
    last_recv,
):
    rows = rhs_ref.shape[0]
    width = inv.shape[-1]
    slots = panel_ref.shape[0]
    tiles = pattern_ref.shape[2]
    tile = width // tiles
    span = NV * rows
    few = rhs_ref.shape[1] // NV
    f32, bf16 = jnp.float32, jnp.bfloat16
    root, top = nodes - 1, nodes // 2 - 1

    s = lax.axis_index("lvl")
    c = lax.axis_index("col")
    y, v = c // NV, c % NV
    x, core = v // 2, v % 2
    other = 1 - core

    level = 0
    step = 1
    for e in range(1, slots + 1):
        whole = 1 - ((s + 1) % 2**e + 2**e - 1) // 2**e
        level = level + whole
        step = step + whole * 2 ** (e - 1)
    side = (s // (2 * step)) % 2
    parent = (s + step * (1 - 2 * side)) % nodes
    above_at = [parent]
    for k in range(1, slots):
        far = step * 2**k
        above_at.append(
            (above_at[-1] + far * (1 - 2 * ((above_at[-1] // (2 * far)) % 2)) + nodes) % nodes
        )
    left = (s + nodes - step // 2) % nodes
    right = (s + step // 2) % nodes
    one_root = (s + 1) // nodes
    one_top = (level + 1) // slots - one_root
    inner = s % 2
    is_root = one_root == 1
    is_top = one_top == 1
    not_root = one_root == 0
    is_leaf = inner == 0
    has_kids = inner * (1 - one_root) == 1
    has_parent = one_root + one_top == 0

    def chip(yy, xx, cc):
        return (yy * NX + xx) * 2 + cc

    own_span = pl.ds(pl.multiple_of(y * span, 128), span)

    barrier = pltpu.get_barrier_semaphore()

    def greet(lvl, col):
        pl.semaphore_signal(barrier, inc=1, device_id=(lvl, col), device_id_type=MESH)

    @pl.when(is_leaf)
    def _():
        for d in range(1, NY * NV):
            greet(s, (c + d) % (NY * NV))

    @pl.when(inner == 1)
    def _():
        for d in range(1, NV):
            greet(s, y * NV + (v + d) % NV)
        for d in range(1, NY):
            greet(s, (y + d) % NY * NV + v)

    @pl.when(has_parent)
    def _():
        for w in range(NY):
            greet(parent, w * NV + v)

    @pl.when(has_kids)
    def _():
        for w in range(NY):
            greet(left, w * NV + v)
            greet(right, w * NV + v)

    @pl.when(is_top)
    def _():
        for q in range(NV):
            greet(root, y * NV + q)

    @pl.when(is_root)
    def _():
        for q in range(NV):
            greet(top, y * NV + q)

    def below(t):
        return [i for i in range(2 ** (t + 1) - 1) if i != 2**t - 1]

    for t in range(2, slots):

        @pl.when(level == t)
        def _(t=t):
            for i in below(t):
                if (i + 1) % 2 ** (t - 1):
                    greet((s + nodes - 2**t + 1 + i) % nodes, c)

    far_count = 0
    for k in range(2, slots):
        far_count = far_count + (slots - 1 - level + slots - k) // slots

    loads = (
        pltpu.make_async_copy(rhs_ref, rhs_own, load_sem.at[0]),
        pltpu.make_async_copy(inverse_ref, inv.at[y, x, core], load_sem.at[1]),
        pltpu.make_async_copy(pattern_ref, pattern_own, load_sem.at[2]),
        pltpu.make_async_copy(panel_ref, panel_own, load_sem.at[3]),
    )
    for load in loads:
        load.start()
    piece = 16

    def mask_slot(k):
        for q in range(rows // piece):
            tile_row = (c * rows + q * piece) // tile
            for j in range(tiles):
                keep = pattern_own[k, tile_row, j].astype(f32)
                part = (slice(q * piece, (q + 1) * piece), slice(j * tile, (j + 1) * tile))
                block = panel_own[(k,) + part]
                factor[(k, x, core) + part] = (block.astype(f32) * keep).astype(bf16)

    loads[0].wait()
    padded = jnp.concatenate(
        [rhs_own[...], jnp.zeros((128 - rows, rhs_ref.shape[1]), f32)], axis=0
    )
    turned[...] = padded.T.reshape(NV, few, 128)
    rhs_in[v] = turned[v]
    loads[1].wait()

    pl.semaphore_wait(
        barrier,
        (NV - 1 + NY - 1) * inner
        + (NV * NY - 1) * (1 - inner)
        + NY * (1 - one_root - one_top)
        + 2 * NY * inner * (1 - one_root)
        + NV * (one_top + one_root)
        + far_count,
    )

    last = slots + 1

    def block(g, xx, cc):
        if g == 0:
            return inv.at[y, xx, cc]
        if g == last:
            return top_inv.at[xx, cc]
        return factor.at[g - 1, xx, cc]

    def gx_copy(g, i):
        if i == 0:
            ref, col = block(g, x, core), chip(y, x, other)
        elif i < NX:
            ref, col = block(g, x, core), chip(y, (x + i) % NX, core)
        else:
            ref, col = block(g, (x + 2 * NX - 1 - i) % NX, core), chip(y, x, other)
        return remote(ref, ref, gx_send.at[g, i], gx_recv.at[g, i], s, col)

    def gx_wait(g, i):
        if i == 0:
            ref = block(g, x, other)
        elif i < NX:
            ref = block(g, (x + NX - i) % NX, core)
        else:
            ref = block(g, (x + 2 * NX - 1 - i) % NX, other)
        arrived(ref, gx_recv.at[g, i])

    def gx_start(g):
        for i in ORDER + (0,):
            gx_copy(g, i).start()

    def gx_pass(g, then=None):
        for i in ORDER:
            gx_wait(g, i)
            gx_copy(g, i + NX - 1).start()
            if then is not None:
                then(NX - i)

    def gx_finish(g):
        for i in (0,) + tuple(i + NX - 1 for i in ORDER):
            gx_wait(g, i)

    def each_y(body):
        for yy in range(NY):

            @pl.when(y == yy)
            def _(yy=yy):
                body(yy)

    def gy_copy(yy, d, j):
        ref = inv.at[yy, (x + j) % NX, core, :, yy * span :]
        col = chip((yy + d) % NY, x, core)
        return remote(ref, ref, gy_send.at[d, j], gy_recv.at[d, j], s, col)

    def gs_copy(yy, d):
        source = (yy + NY - d) % NY
        ref = inv.at[source, :, core, :, source * span :]
        return remote(ref, ref, gs_send.at[d], gs_recv.at[d], s, chip(yy, x, other))

    def gy_start(j):
        def body(yy):
            for d in ORDER:
                gy_copy(yy, d, j).start()

        each_y(body)

    def gy_pass():
        def body(yy):
            for d in ORDER:
                source = (yy + NY - d) % NY
                for j in range(NX):
                    arrived(
                        inv.at[source, (x + j) % NX, core, :, source * span :], gy_recv.at[d, j]
                    )
                gs_copy(yy, d).start()

        each_y(body)

    def gy_finish():
        def body(yy):
            for d in ORDER:
                source = (yy + NY - d) % NY
                arrived(inv.at[source, :, other, :, source * span :], gs_recv.at[d])

        each_y(body)

    def rhs_copy(d):
        to = (v + d) % NV
        return remote(turned.at[to], rhs_in.at[v], rhs_send.at[d], rhs_recv.at[d], s, y * NV + to)

    def row_copy(d):
        ref = rhs_all.at[:, own_span]
        return remote(ref, ref, row_send.at[d], row_recv.at[d], s, (y + d) % NY * NV + v)

    lane = lax.broadcasted_iota(jnp.int32, (few, 128), 1)

    def join_rhs():
        for d in range(1, NV):
            arrived(rhs_in.at[(v + NV - d) % NV], rhs_recv.at[d])
        joined = [jnp.zeros((few, 128), f32) for _ in range(span // 128)]
        for q in range(NV):
            a, b = divmod(q * rows, 128)
            moved = pltpu.roll(rhs_in[q], b, axis=1) if b else rhs_in[q]
            if b + rows <= 128:
                joined[a] = joined[a] + moved
            else:
                joined[a] = joined[a] + jnp.where(lane >= b, moved, 0.0)
                joined[a + 1] = joined[a + 1] + jnp.where(lane >= b, 0.0, moved)
        rhs_all[:, own_span] = jnp.concatenate(joined, axis=1)

    def share_copy(d):
        ref = shares.at[y]
        return remote(ref, ref, share_send.at[d], share_recv.at[d], s, (y + d) % NY * NV + v)

    def share_start(residual, rows_of):
        product = jnp.dot(residual, rows_of.reshape(span, width), preferred_element_type=f32)
        shares[y] = product.astype(bf16)
        for d in ORDER:
            share_copy(d).start()

    def share_sum():
        for d in ORDER:
            arrived(shares.at[(y + NY - d) % NY], share_recv.at[d])
        summed = shares[0].astype(f32)
        for w in range(1, NY):
            summed = summed + shares[w].astype(f32)
        return summed

    def up0_copy(w):
        return remote(
            push.at[0],
            first_in.at[side, :, own_span],
            up0_send.at[w],
            up0_recv.at[side, y],
            parent,
            w * NV + v,
        )

    def leaf_copy():
        return remote(
            push.at[0],
            first_in.at[side, :, own_span],
            up0_send.at[0],
            up0_recv.at[side, y],
            parent,
            c,
        )

    def up_copy(k):
        return remote(
            push.at[k],
            later_in.at[s % (step * 2 ** (k + 1))],
            up_send.at[k],
            up_recv.at[s % (step * 2 ** (k + 1))],
            above_at[k - 1],
            y * NV + v,
        )

    def flat(k):
        return factor[k].reshape(span, width)

    def pushed(k, sample_half):
        return lax.dot_general(sample_half, flat(k), NT, preferred_element_type=f32)

    def cut_pieces(ref, value):
        parts = [value[:, 128 * a : 128 * (a + 1)] for a in range(span // 128)]
        for q in range(NV):
            a, b = divmod(q * rows, 128)
            moved = pltpu.roll(parts[a], 128 - b, axis=1) if b else parts[a]
            if b + rows > 128:
                after = pltpu.roll(parts[a + 1], 128 - b, axis=1)
                moved = jnp.where(lane < 128 - b, moved, after)
            ref[q] = moved.astype(ref.dtype)

    def sample_copy(d):
        to = (v + d) % NV
        return remote(
            piece_out.at[to], sample_in.at[v], sample_send.at[d], sample_recv.at[d], s, y * NV + to
        )

    def solved_copy(d):
        to = (v + d) % NV
        return remote(
            solved_out.at[to], solved_in.at[v], solved_send.at[d], solved_recv.at[d], s, y * NV + to
        )

    def last_copy(d):
        to = (c + d) % (NY * NV)
        return remote(
            last_out.at[to // NV, to % NV],
            last_in.at[c],
            last_send.at[d],
            last_recv.at[d],
            s,
            to,
        )

    def top_copy(i, d):
        to = (v + d) % NV
        ref, sem = (sample_in, sample_recv) if i == 0 else (solved_in, solved_recv)
        return remote(
            top_piece.at[i, to], ref.at[v], top_send.at[i, d], sem.at[d], root, y * NV + to
        )

    def sample_out():
        cut_pieces(piece_out, sample_t[:, own_span])
        sample_in[v] = piece_out[v]
        for d in range(1, NV):
            sample_copy(d).start()

    def move_inv():
        return remote(
            inv.at[y, x, core], top_inv.at[x, core], move_send.at[0], move_recv.at[0], top, c
        )

    def move_rhs():
        return remote(
            rhs_all.at[:, own_span], top_rhs, move_send.at[1], move_recv.at[1], top, c
        )

    def down_copy(k, child, i):
        return remote(
            above.at[k],
            above.at[k + 1],
            down_send.at[i, k],
            down_recv.at[k + 1],
            child,
            y * NV + v,
        )

    def down0_copy(w, child, i):
        return remote(
            part_out.at[w],
            parent_in.at[y],
            down0_send.at[i, w],
            down0_recv.at[y],
            child,
            w * NV + v,
        )

    def own_copy(d):
        to = (y + d) % NY
        return remote(part_out.at[to], own_in.at[y], own_send.at[d], own_recv.at[d], s, to * NV + v)

    def hand_down(k):
        @pl.when(has_kids)
        def _():
            down_copy(k, left, 0).start()
            down_copy(k, right, 1).start()

    def make_joint(k):
        for w in range(NY):
            start = w * span
            joint[k, :, start : start + span] = lax.dot_general(
                factor[k, :, :, :, start:].reshape(span, width - start),
                inv[w, :, :, :, start:].reshape(span, width - start),
                NT,
                preferred_element_type=f32,
            ).astype(bf16)

    def make_base():
        group = lax.broadcasted_iota(jnp.int32, (few, width), 1) // span
        total[...] = jnp.where(group == y, sample_t[...], 0.0)
        for k in range(slots - 1, 1, -1):

            @pl.when(level + k < slots)
            def _():
                arrived(above.at[k], down_recv.at[k])
                if k < slots - 1:
                    hand_down(k)
                total[...] -= jnp.dot(above[k], flat(k), preferred_element_type=f32)

        back = total[...].astype(bf16)
        for w in range(NY):
            start = w * span
            total[:, start : start + span] = lax.dot_general(
                back[:, start:],
                inv[w, :, :, :, start:].reshape(span, width - start),
                NT,
                preferred_element_type=f32,
            )

    @pl.when(is_leaf)
    def _():
        gx_start(0)
        for d in range(1, NV):
            rhs_copy(d).start()
        loads[2].wait()
        loads[3].wait()
        for k in range(slots):
            mask_slot(k)
            if k == 0:
                gx_start(1)
        gx_pass(0, lambda j: gx_start(2) if j == 3 and slots > 1 else None)
        join_rhs()
        gx_finish(0)
        share_start(rhs_all[:, own_span].astype(bf16), inv[y])
        gx_pass(1, lambda j: gx_start(3) if j == 3 and slots > 2 else None)
        sample_t[...] = share_sum()
        sample_half = sample_t[...].astype(bf16)
        for k in range(slots):
            if k > 0:
                gx_pass(
                    k + 1, lambda j: gx_start(k + 3) if j == 3 and k + 3 <= slots else None
                )
            gx_finish(k + 1)
            push[k] = pushed(k, sample_half).astype(bf16)
            if k == 0:
                leaf_copy().start()
            else:
                up_copy(k).start()
        for j in range(NX):
            gy_start(j)
        sample_out()
        gy_pass()
        gy_finish()
        make_joint(0)
        if slots > 1:
            make_joint(1)

    @pl.when(inner == 1)
    def _():
        @pl.when(is_root)
        def _():
            move_inv().start()

        @pl.when(not_root)
        def _():
            gx_start(0)
            gy_start(0)

        for d in range(1, NV):
            rhs_copy(d).start()
        loads[2].wait()
        loads[3].wait()
        for k in range(max(slots - 1, 1)):
            mask_slot(k)

        @pl.when(not_root)
        def _():
            def follow(j):
                gy_start(j)
                if j == 3:
                    gx_start(1)

            gx_pass(0, follow)

        join_rhs()

        @pl.when(is_root)
        def _():
            move_rhs().start()

        @pl.when(not_root)
        def _():
            for d in range(1, NY):
                row_copy(d).start()
            gx_pass(1)
            for k in range(1, slots - 1):

                @pl.when(level + k < slots)
                def _():
                    gx_start(k + 1)

            @pl.when(is_top)
            def _():
                arrived(top_inv.at[x, core], move_recv.at[0])
                gx_start(last)

            def rest_of_inverse():
                gy_pass()
                for d in range(1, NY):
                    group_of = (y + NY - d) % NY
                    arrived(
                        rhs_all.at[:, pl.ds(pl.multiple_of(group_of * span, 128), span)],
                        row_recv.at[d],
                    )
                gy_finish()

            @pl.when(level == 1)
            def _():
                gx_finish(0)
                for i in range(2):
                    arrived(first_in.at[i, :, own_span], up0_recv.at[i, y])
                incoming = first_in[0, :, own_span].astype(f32) + first_in[
                    1, :, own_span
                ].astype(f32)
                share_start((rhs_all[:, own_span] - incoming).astype(bf16), inv[y])
                gx_finish(1)
                sample_t[...] = share_sum()

            @pl.when(level > 1)
            def _():
                rest_of_inverse()
                gx_finish(0)
                gx_finish(1)

                @pl.when(is_top)
                def _():
                    gx_pass(last)
                    gx_finish(last)
                    arrived(top_rhs, move_recv.at[1])
                    make_joint(0)

                for i in range(2):
                    for w in range(NY):
                        arrived(first_in.at[i, :, w * span : (w + 1) * span], up0_recv.at[i, w])
                incoming = first_in[0].astype(f32) + first_in[1].astype(f32)
                residual = (rhs_all[...] - incoming).astype(bf16)
                for w in range(NY):
                    to = (w + 1) * span
                    sample_t[:, w * span : to] = jnp.dot(
                        residual[:, :to],
                        inv[: w + 1, :, :, :, w * span : to].reshape(to, span),
                        preferred_element_type=f32,
                    )

            sample_half = sample_t[...].astype(bf16)

            def pushed_sum(t):
                out = pushed(0, sample_half)
                for i in below(t):
                    arrived(later_in.at[i], up_recv.at[i])
                    out = out + later_in[i].astype(f32)
                return out

            for t in range(1, slots - 1):

                @pl.when(level == t)
                def _(t=t):
                    push[0] = pushed_sum(t).astype(bf16)
                    for w in range(NY):
                        up0_copy(w).start()

            @pl.when(is_top)
            def _():
                residual_root = (top_rhs[...] - pushed_sum(slots - 1)).astype(bf16)
                share_start(residual_root, top_inv[...])
                make_base()
                root_t = share_sum()
                root_sample[...] = root_t
                solved_root = lax.dot_general(
                    root_t.astype(bf16),
                    top_inv[...].reshape(span, width),
                    NT,
                    preferred_element_type=f32,
                )
                root_solved[...] = solved_root
                above[0] = solved_root.astype(bf16)
                down_copy(0, left, 0).start()
                down_copy(0, right, 1).start()

            for k in range(1, slots - 1):

                @pl.when(level + k < slots)
                def _():
                    gx_pass(k + 1)
                    gx_finish(k + 1)
                    push[k] = pushed(k, sample_half).astype(bf16)
                    up_copy(k).start()

            @pl.when(has_parent)
            def _():
                sample_out()

                @pl.when(level == 1)
                def _():
                    rest_of_inverse()

                make_joint(0)
                if slots > 1:
                    make_joint(1)

    @pl.when(not_root)
    def _():
        @pl.when(has_parent)
        def _():
            make_base()

            @pl.when(level + 1 < slots)
            def _():
                arrived(above.at[1], down_recv.at[1])
                hand_down(1)
                total[...] -= jnp.dot(above[1], joint[1], preferred_element_type=f32)

            for w in range(NY):
                arrived(parent_in.at[w], down0_recv.at[w])
            summed = parent_in[0].astype(f32)
            for w in range(1, NY):
                summed = summed + parent_in[w].astype(f32)
            above[0] = summed.astype(bf16)
            hand_down(0)

        for w in range(NY):
            lanes = slice(w * span, (w + 1) * span)
            part = total[:, lanes] - jnp.dot(
                above[0], joint[0, :, lanes], preferred_element_type=f32
            )
            part_out[w] = part.astype(bf16)

            @pl.when(is_leaf)
            def _():
                cut_pieces(last_out.at[w], part)

            @pl.when(has_kids)
            def _():
                down0_copy(w, left, 0).start()
                down0_copy(w, right, 1).start()

        @pl.when(is_leaf)
        def _():
            last_in[c] = last_out[y, v]
            for d in range(1, NY * NV):
                last_copy(d).start()

        @pl.when(has_kids)
        def _():
            own_in[y] = part_out[y]
            for d in ORDER:
                own_copy(d).start()

        @pl.when(is_top)
        def _():
            cut_pieces(top_piece.at[0], root_sample[:, own_span])
            cut_pieces(top_piece.at[1], root_solved[...])
            for d in range(NV):
                top_copy(0, d).start()
                top_copy(1, d).start()
            sample_out()

        for d in range(1, NV):
            arrived(sample_in.at[(v + NV - d) % NV], sample_recv.at[d])
        sample_ref[...] = sample_in[...].reshape(NV * few, 128).T[:rows, :]

        @pl.when(has_kids)
        def _():
            for d in ORDER:
                arrived(own_in.at[(y + NY - d) % NY], own_recv.at[d])
            solved = own_in[0].astype(f32)
            for w in range(1, NY):
                solved = solved + own_in[w].astype(f32)
            cut_pieces(solved_out, solved)
            solved_in[v] = solved_out[v]
            for d in range(1, NV):
                solved_copy(d).start()
            for d in range(1, NV):
                arrived(solved_in.at[(v + NV - d) % NV], solved_recv.at[d])
            answer_ref[...] = solved_in[...].reshape(NV * few, 128).T[:rows, :]

        @pl.when(is_leaf)
        def _():
            for d in range(1, NY * NV):
                source = (c + NY * NV - d) % (NY * NV)
                arrived(last_in.at[source], last_recv.at[d])
            pieces = last_in[0:NV].astype(f32)
            for w in range(1, NY):
                pieces = pieces + last_in[w * NV : (w + 1) * NV].astype(f32)
            answer_ref[...] = pieces.reshape(NV * few, 128).T[:rows, :]

    @pl.when(is_root)
    def _():
        for d in range(NV):
            arrived(sample_in.at[(v + NV - d) % NV], sample_recv.at[d])
            arrived(solved_in.at[(v + NV - d) % NV], solved_recv.at[d])
        sample_ref[...] = sample_in[...].reshape(NV * few, 128).T[:rows, :]
        answer_ref[...] = solved_in[...].reshape(NV * few, 128).T[:rows, :]

    for d in range(1, NV):
        rhs_copy(d).wait_send()

    def gx_sent(g):
        for i in range(2 * NX - 1):
            gx_copy(g, i).wait_send()

    @pl.when(is_root)
    def _():
        move_inv().wait_send()
        move_rhs().wait_send()

    @pl.when(not_root)
    def _():
        gx_sent(0)
        for k in range(slots):

            @pl.when(level + k < slots)
            def _():
                gx_sent(k + 1)

        def gy_sent(yy):
            for d in ORDER:
                for j in range(NX):
                    gy_copy(yy, d, j).wait_send()
                gs_copy(yy, d).wait_send()

        each_y(gy_sent)
        for d in range(1, NV):
            sample_copy(d).wait_send()

    @pl.when(has_kids)
    def _():
        for d in range(1, NV):
            solved_copy(d).wait_send()
        for d in ORDER:
            own_copy(d).wait_send()
        for d in range(1, NY):
            row_copy(d).wait_send()
        for i, child in enumerate((left, right)):
            for w in range(NY):
                down0_copy(w, child, i).wait_send()
            for k in range(slots - 1):

                @pl.when(level + k < slots)
                def _():
                    down_copy(k, child, i).wait_send()

    @pl.when(has_parent)
    def _():
        @pl.when(inner == 1)
        def _():
            for w in range(NY):
                up0_copy(w).wait_send()

        for k in range(1, slots):

            @pl.when(level + k < slots)
            def _():
                up_copy(k).wait_send()

    def share_sent():
        for d in ORDER:
            share_copy(d).wait_send()

    @pl.when(is_leaf)
    def _():
        share_sent()
        leaf_copy().wait_send()
        for d in range(1, NY * NV):
            last_copy(d).wait_send()

    @pl.when(level == 1)
    def _():
        share_sent()

    @pl.when(is_top)
    def _():
        share_sent()
        gx_sent(last)
        for d in range(NV):
            top_copy(0, d).wait_send()
            top_copy(1, d).wait_send()


def on_device(nodes, rhs, panel, inverse_t, pattern):
    rows, count = rhs.shape[1:]
    slots = panel.shape[1]
    width = inverse_t.shape[2]
    span = NV * rows
    few = count // NV
    f32, bf16 = jnp.float32, jnp.bfloat16
    dma = pltpu.SemaphoreType.DMA
    vmem = pl.BlockSpec(memory_space=pltpu.VMEM)
    outs = pl.pallas_call(
        functools.partial(kernel, nodes),
        out_shape=[jax.ShapeDtypeStruct((rows, count), f32)] * 2,
        in_specs=[pl.BlockSpec(memory_space=pltpu.HBM)] * 4,
        out_specs=[vmem, vmem],
        scratch_shapes=[
            pltpu.VMEM((rows, count), f32),
            pltpu.VMEM((slots, rows, width), bf16),
            pltpu.SMEM(pattern.shape[1:], jnp.int32),
            pltpu.VMEM((slots, NX, 2, rows, width), bf16),
            pltpu.VMEM((NY, NX, 2, rows, width), bf16),
            pltpu.VMEM((NX, 2, rows, width), bf16),
            pltpu.VMEM((NV, few, 128), f32),
            pltpu.VMEM((NV, few, 128), f32),
            pltpu.VMEM((few, width), f32),
            pltpu.VMEM((few, span), f32),
            pltpu.VMEM((2, few, width), bf16),
            pltpu.VMEM((2**slots - 1, few, span), bf16),
            pltpu.VMEM((slots, few, span), bf16),
            pltpu.VMEM((NY, few, width), bf16),
            pltpu.VMEM((few, width), f32),
            pltpu.VMEM((few, width), f32),
            pltpu.VMEM((NV, few, 128), f32),
            pltpu.VMEM((NV, few, 128), f32),
            pltpu.VMEM((NY, few, span), bf16),
            pltpu.VMEM((slots, few, span), bf16),
            pltpu.VMEM((NY, few, span), bf16),
            pltpu.VMEM((NY, few, span), bf16),
            pltpu.VMEM((NV, few, 128), f32),
            pltpu.VMEM((NV, few, 128), f32),
            pltpu.VMEM((2, NV, few, 128), f32),
            pltpu.VMEM((few, width), f32),
            pltpu.VMEM((few, span), f32),
        ]
        + [dma((slots + 2, 2 * NX - 1))] * 2
        + [dma((NY, NX))] * 2
        + [dma((NY,))] * 2
        + [dma((NV,))] * 2
        + [dma((NY,))] * 2
        + [dma((NY,))] * 2
        + [dma((NY,)), dma((2, NY))]
        + [dma((slots,)), dma((2**slots - 1,))]
        + [dma((2, NY)), dma((NY,))]
        + [dma((2, slots)), dma((slots,))]
        + [dma((NY,))] * 2
        + [dma((NV,))] * 4
        + [dma((2,))] * 2
        + [dma((2, NV))]
        + [dma((4,)), pltpu.VMEM((2, span, width), bf16)]
        + [pltpu.VMEM((NY, NV, few, 128), bf16), pltpu.VMEM((NY * NV, few, 128), bf16)]
        + [dma((NY * NV,))] * 2,
        compiler_params=pltpu.CompilerParams(
            collective_id=0, has_side_effects=True, vmem_limit_bytes=56 * 2**20
        ),
    )(rhs[0], panel[0], inverse_t[0], pattern[0])
    return outs[0][None], outs[1][None]


def solution(mesh):
    in_specs = (
        P("lvl", "col", None),
        P("lvl", None, "col", None),
        P("lvl", "col", None),
        P("lvl", None, None, None),
    )
    out_specs = (P("lvl", "col", None), P("lvl", "col", None))
    return jax.shard_map(
        functools.partial(on_device, mesh.shape["lvl"]),
        mesh=mesh,
        in_specs=in_specs,
        out_specs=out_specs,
        check_vma=False,
    )
```

```python
import functools

import jax
import jax.numpy as jnp
from jax import lax
from jax.experimental import pallas as pl
from jax.experimental.pallas import tpu as pltpu
from jax.sharding import PartitionSpec as P

MESH = pl.DeviceIdType.MESH
NT = (((1,), (1,)), ((), ()))
NX = 4
NY = 4
NV = 2 * NX
ORDER = (1, 3, 2)


def remote(src, dst, send_sem, recv_sem, lvl, col):
    return pltpu.make_async_remote_copy(
        src_ref=src,
        dst_ref=dst,
        send_sem=send_sem,
        recv_sem=recv_sem,
        device_id=(lvl, col),
        device_id_type=MESH,
    )


def arrived(dst, sem):
    pltpu.make_async_copy(dst, dst, sem).wait()


def kernel(
    nodes,
    rhs_ref,
    panel_ref,
    inverse_ref,
    pattern_ref,
    sample_ref,
    answer_ref,
    rhs_own,
    panel_own,
    pattern_own,
    factor,
    inv,
    top_inv,
    turned,
    rhs_in,
    rhs_all,
    top_rhs,
    first_in,
    later_in,
    push,
    shares,
    sample_t,
    total,
    piece_out,
    sample_in,
    parent_in,
    above,
    part_out,
    own_in,
    solved_out,
    solved_in,
    top_piece,
    root_sample,
    root_solved,
    gx_send,
    gx_recv,
    gy_send,
    gy_recv,
    gs_send,
    gs_recv,
    rhs_send,
    rhs_recv,
    row_send,
    row_recv,
    share_send,
    share_recv,
    up0_send,
    up0_recv,
    up_send,
    up_recv,
    down0_send,
    down0_recv,
    down_send,
    down_recv,
    own_send,
    own_recv,
    sample_send,
    sample_recv,
    solved_send,
    solved_recv,
    move_send,
    move_recv,
    top_send,
    load_sem,
    joint,
    last_out,
    last_in,
    last_send,
    last_recv,
):
    rows = rhs_ref.shape[0]
    width = inv.shape[-1]
    slots = panel_ref.shape[0]
    tiles = pattern_ref.shape[2]
    tile = width // tiles
    span = NV * rows
    few = rhs_ref.shape[1] // NV
    f32, bf16 = jnp.float32, jnp.bfloat16
    root, top = nodes - 1, nodes // 2 - 1

    s = lax.axis_index("lvl")
    c = lax.axis_index("col")
    y, v = c // NV, c % NV
    x, core = v // 2, v % 2
    other = 1 - core

    level = 0
    step = 1
    for e in range(1, slots + 1):
        whole = 1 - ((s + 1) % 2**e + 2**e - 1) // 2**e
        level = level + whole
        step = step + whole * 2 ** (e - 1)
    side = (s // (2 * step)) % 2
    parent = (s + step * (1 - 2 * side)) % nodes
    above_at = [parent]
    for k in range(1, slots):
        far = step * 2**k
        above_at.append(
            (above_at[-1] + far * (1 - 2 * ((above_at[-1] // (2 * far)) % 2)) + nodes) % nodes
        )
    left = (s + nodes - step // 2) % nodes
    right = (s + step // 2) % nodes
    one_root = (s + 1) // nodes
    one_top = (level + 1) // slots - one_root
    inner = s % 2
    is_root = one_root == 1
    is_top = one_top == 1
    not_root = one_root == 0
    is_leaf = inner == 0
    has_kids = inner * (1 - one_root) == 1
    has_parent = one_root + one_top == 0

    def chip(yy, xx, cc):
        return (yy * NX + xx) * 2 + cc

    own_span = pl.ds(pl.multiple_of(y * span, 128), span)

    barrier = pltpu.get_barrier_semaphore()

    def greet(lvl, col):
        pl.semaphore_signal(barrier, inc=1, device_id=(lvl, col), device_id_type=MESH)

    @pl.when(is_leaf)
    def _():
        for d in range(1, NY * NV):
            greet(s, (c + d) % (NY * NV))

    @pl.when(inner == 1)
    def _():
        for d in range(1, NV):
            greet(s, y * NV + (v + d) % NV)
        for d in range(1, NY):
            greet(s, (y + d) % NY * NV + v)

    @pl.when(has_parent)
    def _():
        for w in range(NY):
            greet(parent, w * NV + v)

    @pl.when(has_kids)
    def _():
        for w in range(NY):
            greet(left, w * NV + v)
            greet(right, w * NV + v)

    @pl.when(is_top)
    def _():
        for q in range(NV):
            greet(root, y * NV + q)

    @pl.when(is_root)
    def _():
        for q in range(NV):
            greet(top, y * NV + q)

    def below(t):
        return [i for i in range(2 ** (t + 1) - 1) if i != 2**t - 1]

    for t in range(2, slots):

        @pl.when(level == t)
        def _(t=t):
            for i in below(t):
                if (i + 1) % 2 ** (t - 1):
                    greet((s + nodes - 2**t + 1 + i) % nodes, c)

    far_count = 0
    for k in range(2, slots):
        far_count = far_count + (slots - 1 - level + slots - k) // slots

    loads = (
        pltpu.make_async_copy(rhs_ref, rhs_own, load_sem.at[0]),
        pltpu.make_async_copy(inverse_ref, inv.at[y, x, core], load_sem.at[1]),
        pltpu.make_async_copy(pattern_ref, pattern_own, load_sem.at[2]),
        pltpu.make_async_copy(panel_ref, panel_own, load_sem.at[3]),
    )
    for load in loads:
        load.start()
    piece = 16

    def mask_slot(k):
        for q in range(rows // piece):
            tile_row = (c * rows + q * piece) // tile
            for j in range(tiles):
                keep = pattern_own[k, tile_row, j].astype(f32)
                part = (slice(q * piece, (q + 1) * piece), slice(j * tile, (j + 1) * tile))
                block = panel_own[(k,) + part]
                factor[(k, x, core) + part] = (block.astype(f32) * keep).astype(bf16)

    loads[0].wait()
    padded = jnp.concatenate(
        [rhs_own[...], jnp.zeros((128 - rows, rhs_ref.shape[1]), f32)], axis=0
    )
    turned[...] = padded.T.reshape(NV, few, 128)
    rhs_in[v] = turned[v]
    loads[1].wait()

    pl.semaphore_wait(
        barrier,
        (NV - 1 + NY - 1) * inner
        + (NV * NY - 1) * (1 - inner)
        + NY * (1 - one_root - one_top)
        + 2 * NY * inner * (1 - one_root)
        + NV * (one_top + one_root)
        + far_count,
    )

    last = slots + 1

    def block(g, xx, cc):
        if g == 0:
            return inv.at[y, xx, cc]
        if g == last:
            return top_inv.at[xx, cc]
        return factor.at[g - 1, xx, cc]

    def gx_copy(g, i):
        if i == 0:
            ref, col = block(g, x, core), chip(y, x, other)
        elif i < NX:
            ref, col = block(g, x, core), chip(y, (x + i) % NX, core)
        else:
            ref, col = block(g, (x + 2 * NX - 1 - i) % NX, core), chip(y, x, other)
        return remote(ref, ref, gx_send.at[g, i], gx_recv.at[g, i], s, col)

    def gx_wait(g, i):
        if i == 0:
            ref = block(g, x, other)
        elif i < NX:
            ref = block(g, (x + NX - i) % NX, core)
        else:
            ref = block(g, (x + 2 * NX - 1 - i) % NX, other)
        arrived(ref, gx_recv.at[g, i])

    def gx_start(g):
        for i in ORDER + (0,):
            gx_copy(g, i).start()

    def gx_pass(g, then=None):
        for i in ORDER:
            gx_wait(g, i)
            gx_copy(g, i + NX - 1).start()
            if then is not None:
                then(NX - i)

    def gx_finish(g):
        for i in (0,) + tuple(i + NX - 1 for i in ORDER):
            gx_wait(g, i)

    def each_y(body):
        for yy in range(NY):

            @pl.when(y == yy)
            def _(yy=yy):
                body(yy)

    def gy_copy(yy, d, j):
        ref = inv.at[yy, (x + j) % NX, core, :, yy * span :]
        col = chip((yy + d) % NY, x, core)
        return remote(ref, ref, gy_send.at[d, j], gy_recv.at[d, j], s, col)

    def gs_copy(yy, d):
        source = (yy + NY - d) % NY
        ref = inv.at[source, :, core, :, source * span :]
        return remote(ref, ref, gs_send.at[d], gs_recv.at[d], s, chip(yy, x, other))

    def gy_start(j):
        def body(yy):
            for d in ORDER:
                gy_copy(yy, d, j).start()

        each_y(body)

    def gy_pass():
        def body(yy):
            for d in ORDER:
                source = (yy + NY - d) % NY
                for j in range(NX):
                    arrived(
                        inv.at[source, (x + j) % NX, core, :, source * span :], gy_recv.at[d, j]
                    )
                gs_copy(yy, d).start()

        each_y(body)

    def gy_finish():
        def body(yy):
            for d in ORDER:
                source = (yy + NY - d) % NY
                arrived(inv.at[source, :, other, :, source * span :], gs_recv.at[d])

        each_y(body)

    def rhs_copy(d):
        to = (v + d) % NV
        return remote(turned.at[to], rhs_in.at[v], rhs_send.at[d], rhs_recv.at[d], s, y * NV + to)

    def row_copy(d):
        ref = rhs_all.at[:, own_span]
        return remote(ref, ref, row_send.at[d], row_recv.at[d], s, (y + d) % NY * NV + v)

    def rows_arrived():
        for d in range(1, NY):
            group_of = (y + NY - d) % NY
            arrived(
                rhs_all.at[:, pl.ds(pl.multiple_of(group_of * span, 128), span)], row_recv.at[d]
            )

    lane = lax.broadcasted_iota(jnp.int32, (few, 128), 1)

    def join_rhs():
        for d in range(1, NV):
            arrived(rhs_in.at[(v + NV - d) % NV], rhs_recv.at[d])
        joined = [jnp.zeros((few, 128), f32) for _ in range(span // 128)]
        for q in range(NV):
            a, b = divmod(q * rows, 128)
            moved = pltpu.roll(rhs_in[q], b, axis=1) if b else rhs_in[q]
            if b + rows <= 128:
                joined[a] = joined[a] + moved
            else:
                joined[a] = joined[a] + jnp.where(lane >= b, moved, 0.0)
                joined[a + 1] = joined[a + 1] + jnp.where(lane >= b, 0.0, moved)
        rhs_all[:, own_span] = jnp.concatenate(joined, axis=1)

    def share_copy(d):
        ref = shares.at[y]
        return remote(ref, ref, share_send.at[d], share_recv.at[d], s, (y + d) % NY * NV + v)

    def share_start(residual, rows_of):
        product = jnp.dot(residual, rows_of.reshape(span, width), preferred_element_type=f32)
        shares[y] = product.astype(bf16)
        for d in ORDER:
            share_copy(d).start()

    def share_sum():
        for d in ORDER:
            arrived(shares.at[(y + NY - d) % NY], share_recv.at[d])
        summed = shares[0].astype(f32)
        for w in range(1, NY):
            summed = summed + shares[w].astype(f32)
        return summed

    def up0_copy(w):
        return remote(
            push.at[0],
            first_in.at[side, :, own_span],
            up0_send.at[w],
            up0_recv.at[side, y],
            parent,
            w * NV + v,
        )

    def leaf_copy():
        return remote(
            push.at[0],
            first_in.at[side, :, own_span],
            up0_send.at[0],
            up0_recv.at[side, y],
            parent,
            c,
        )

    def up_copy(k):
        return remote(
            push.at[k],
            later_in.at[s % (step * 2 ** (k + 1))],
            up_send.at[k],
            up_recv.at[s % (step * 2 ** (k + 1))],
            above_at[k - 1],
            y * NV + v,
        )

    def flat(k):
        return factor[k].reshape(span, width)

    def pushed(k, sample_half):
        return lax.dot_general(sample_half, flat(k), NT, preferred_element_type=f32)

    def cut_pieces(ref, value):
        parts = [value[:, 128 * a : 128 * (a + 1)] for a in range(span // 128)]
        for q in range(NV):
            a, b = divmod(q * rows, 128)
            moved = pltpu.roll(parts[a], 128 - b, axis=1) if b else parts[a]
            if b + rows > 128:
                after = pltpu.roll(parts[a + 1], 128 - b, axis=1)
                moved = jnp.where(lane < 128 - b, moved, after)
            ref[q] = moved.astype(ref.dtype)

    def sample_copy(d):
        to = (v + d) % NV
        return remote(
            piece_out.at[to], sample_in.at[v], sample_send.at[d], sample_recv.at[d], s, y * NV + to
        )

    def solved_copy(d):
        to = (v + d) % NV
        return remote(
            solved_out.at[to], solved_in.at[v], solved_send.at[d], solved_recv.at[d], s, y * NV + to
        )

    def last_copy(d):
        to = (c + d) % (NY * NV)
        return remote(
            last_out.at[to // NV, to % NV],
            last_in.at[c],
            last_send.at[d],
            last_recv.at[d],
            s,
            to,
        )

    def top_copy(i, d):
        to = (v + d) % NV
        ref, sem = (sample_in, sample_recv) if i == 0 else (solved_in, solved_recv)
        return remote(
            top_piece.at[i, to], ref.at[v], top_send.at[i, d], sem.at[d], root, y * NV + to
        )

    def sample_out():
        cut_pieces(piece_out, sample_t[:, own_span])
        sample_in[v] = piece_out[v]
        for d in range(1, NV):
            sample_copy(d).start()

    def move_inv():
        return remote(
            inv.at[y, x, core], top_inv.at[x, core], move_send.at[0], move_recv.at[0], top, c
        )

    def move_rhs():
        return remote(
            rhs_all.at[:, own_span], top_rhs, move_send.at[1], move_recv.at[1], top, c
        )

    def down_copy(k, child, i):
        return remote(
            above.at[k],
            above.at[k + 1],
            down_send.at[i, k],
            down_recv.at[k + 1],
            child,
            y * NV + v,
        )

    def down0_copy(w, child, i):
        return remote(
            part_out.at[w],
            parent_in.at[y],
            down0_send.at[i, w],
            down0_recv.at[y],
            child,
            w * NV + v,
        )

    def own_copy(d):
        to = (y + d) % NY
        return remote(part_out.at[to], own_in.at[y], own_send.at[d], own_recv.at[d], s, to * NV + v)

    def hand_down(k):
        @pl.when(has_kids)
        def _():
            down_copy(k, left, 0).start()
            down_copy(k, right, 1).start()

    def make_joint(k):
        def some_rows(r, carry):
            at = pl.ds(pl.multiple_of(r * 2 * rows, 2 * rows), 2 * rows)
            for w in range(NY):
                start = w * span
                joint[k, at, start : start + span] = lax.dot_general(
                    factor[k, r, :, :, start:].reshape(2 * rows, width - start),
                    inv[w, :, :, :, start:].reshape(span, width - start),
                    NT,
                    preferred_element_type=f32,
                ).astype(bf16)
            return carry

        lax.fori_loop(0, NX, some_rows, 0)

    def make_base():
        group = lax.broadcasted_iota(jnp.int32, (few, width), 1) // span
        total[...] = jnp.where(group == y, sample_t[...], 0.0)
        for k in range(slots - 1, 1, -1):

            @pl.when(level + k < slots)
            def _():
                arrived(above.at[k], down_recv.at[k])
                if k < slots - 1:
                    hand_down(k)
                total[...] -= jnp.dot(above[k], flat(k), preferred_element_type=f32)

        back = total[...].astype(bf16)
        for w in range(NY):
            start = w * span
            total[:, start : start + span] = lax.dot_general(
                back[:, start:],
                inv[w, :, :, :, start:].reshape(span, width - start),
                NT,
                preferred_element_type=f32,
            )

    @pl.when(is_leaf)
    def _():
        gx_start(0)
        for d in range(1, NV):
            rhs_copy(d).start()
        loads[2].wait()
        loads[3].wait()
        for k in range(slots):
            mask_slot(k)
            if k == 0:
                gx_start(1)
        gx_pass(0, lambda j: gx_start(2) if j == 3 and slots > 1 else None)
        join_rhs()
        gx_finish(0)
        share_start(rhs_all[:, own_span].astype(bf16), inv[y])
        gx_pass(1, lambda j: gx_start(3) if j == 3 and slots > 2 else None)
        sample_t[...] = share_sum()
        sample_half = sample_t[...].astype(bf16)
        for k in range(slots):
            if k > 0:
                gx_pass(
                    k + 1, lambda j: gx_start(k + 3) if j == 3 and k + 3 <= slots else None
                )
            gx_finish(k + 1)
            push[k] = pushed(k, sample_half).astype(bf16)
            if k == 0:
                leaf_copy().start()
                for j in range(NX):
                    gy_start(j)
            else:
                up_copy(k).start()

    @pl.when(inner == 1)
    def _():
        @pl.when(is_root)
        def _():
            move_inv().start()

        @pl.when(not_root)
        def _():
            gx_start(0)
            gy_start(0)

        for d in range(1, NV):
            rhs_copy(d).start()
        loads[2].wait()
        loads[3].wait()
        for k in range(max(slots - 1, 1)):
            mask_slot(k)

        @pl.when(not_root)
        def _():
            def follow(j):
                gy_start(j)
                if j == 3:
                    gx_start(1)

            gx_pass(0, follow)

        join_rhs()

        @pl.when(is_root)
        def _():
            move_rhs().start()

        @pl.when(not_root)
        def _():
            for d in range(1, NY):
                row_copy(d).start()
            gx_pass(1)
            for k in range(1, slots - 1):

                @pl.when(level + k < slots)
                def _():
                    gx_start(k + 1)

            @pl.when(is_top)
            def _():
                arrived(top_inv.at[x, core], move_recv.at[0])
                gx_start(last)

            @pl.when(level == 1)
            def _():
                gx_finish(0)
                for i in range(2):
                    arrived(first_in.at[i, :, own_span], up0_recv.at[i, y])
                incoming = first_in[0, :, own_span].astype(f32) + first_in[
                    1, :, own_span
                ].astype(f32)
                share_start((rhs_all[:, own_span] - incoming).astype(bf16), inv[y])
                gx_finish(1)
                sample_t[...] = share_sum()

            @pl.when(level > 1)
            def _():
                gy_pass()
                rows_arrived()
                gy_finish()
                gx_finish(0)
                gx_finish(1)

                @pl.when(is_top)
                def _():
                    gx_pass(last)
                    gx_finish(last)
                    arrived(top_rhs, move_recv.at[1])
                    make_joint(0)

                for i in range(2):
                    for w in range(NY):
                        arrived(first_in.at[i, :, w * span : (w + 1) * span], up0_recv.at[i, w])
                incoming = first_in[0].astype(f32) + first_in[1].astype(f32)
                residual = (rhs_all[...] - incoming).astype(bf16)
                for w in range(NY):
                    to = (w + 1) * span
                    sample_t[:, w * span : to] = jnp.dot(
                        residual[:, :to],
                        inv[: w + 1, :, :, :, w * span : to].reshape(to, span),
                        preferred_element_type=f32,
                    )

            sample_half = sample_t[...].astype(bf16)

            def pushed_sum(t):
                out = pushed(0, sample_half)
                for i in below(t):
                    arrived(later_in.at[i], up_recv.at[i])
                    out = out + later_in[i].astype(f32)
                return out

            for t in range(1, slots - 1):

                @pl.when(level == t)
                def _(t=t):
                    push[0] = pushed_sum(t).astype(bf16)
                    for w in range(NY):
                        up0_copy(w).start()

            @pl.when(is_top)
            def _():
                residual_root = (top_rhs[...] - pushed_sum(slots - 1)).astype(bf16)
                share_start(residual_root, top_inv[...])
                make_base()
                root_t = share_sum()
                root_sample[...] = root_t
                solved_root = lax.dot_general(
                    root_t.astype(bf16),
                    top_inv[...].reshape(span, width),
                    NT,
                    preferred_element_type=f32,
                )
                root_solved[...] = solved_root
                above[0] = solved_root.astype(bf16)
                down_copy(0, left, 0).start()
                down_copy(0, right, 1).start()

            for k in range(1, slots - 1):

                @pl.when(level + k < slots)
                def _():
                    gx_pass(k + 1)
                    gx_finish(k + 1)
                    push[k] = pushed(k, sample_half).astype(bf16)
                    up_copy(k).start()

    @pl.when(has_parent)
    def _():
        sample_out()

        @pl.when(level < 2)
        def _():
            gy_pass()

            @pl.when(level == 1)
            def _():
                rows_arrived()

            gy_finish()

        def one_joint(k, carry):
            make_joint(k)
            return carry

        lax.fori_loop(0, min(slots, 2), one_joint, 0)

    @pl.when(not_root)
    def _():
        @pl.when(has_parent)
        def _():
            make_base()

            @pl.when(level + 1 < slots)
            def _():
                arrived(above.at[1], down_recv.at[1])
                hand_down(1)
                total[...] -= jnp.dot(above[1], joint[1], preferred_element_type=f32)

            for w in range(NY):
                arrived(parent_in.at[w], down0_recv.at[w])
            summed = parent_in[0].astype(f32)
            for w in range(1, NY):
                summed = summed + parent_in[w].astype(f32)
            above[0] = summed.astype(bf16)
            hand_down(0)

        for w in range(NY):
            lanes = slice(w * span, (w + 1) * span)
            part = total[:, lanes] - jnp.dot(
                above[0], joint[0, :, lanes], preferred_element_type=f32
            )
            part_out[w] = part.astype(bf16)

            @pl.when(is_leaf)
            def _():
                cut_pieces(last_out.at[w], part)

            @pl.when(has_kids)
            def _():
                down0_copy(w, left, 0).start()
                down0_copy(w, right, 1).start()

        @pl.when(is_leaf)
        def _():
            last_in[c] = last_out[y, v]
            for d in range(1, NY * NV):
                last_copy(d).start()

        @pl.when(has_kids)
        def _():
            own_in[y] = part_out[y]
            for d in ORDER:
                own_copy(d).start()

        @pl.when(is_top)
        def _():
            cut_pieces(top_piece.at[0], root_sample[:, own_span])
            cut_pieces(top_piece.at[1], root_solved[...])
            for d in range(NV):
                top_copy(0, d).start()
                top_copy(1, d).start()
            sample_out()

        for d in range(1, NV):
            arrived(sample_in.at[(v + NV - d) % NV], sample_recv.at[d])
        sample_ref[...] = sample_in[...].reshape(NV * few, 128).T[:rows, :]

        @pl.when(has_kids)
        def _():
            for d in ORDER:
                arrived(own_in.at[(y + NY - d) % NY], own_recv.at[d])
            solved = own_in[0].astype(f32)
            for w in range(1, NY):
                solved = solved + own_in[w].astype(f32)
            cut_pieces(solved_out, solved)
            solved_in[v] = solved_out[v]
            for d in range(1, NV):
                solved_copy(d).start()
            for d in range(1, NV):
                arrived(solved_in.at[(v + NV - d) % NV], solved_recv.at[d])
            answer_ref[...] = solved_in[...].reshape(NV * few, 128).T[:rows, :]

        @pl.when(is_leaf)
        def _():
            for d in range(1, NY * NV):
                source = (c + NY * NV - d) % (NY * NV)
                arrived(last_in.at[source], last_recv.at[d])
            pieces = last_in[0:NV].astype(f32)
            for w in range(1, NY):
                pieces = pieces + last_in[w * NV : (w + 1) * NV].astype(f32)
            answer_ref[...] = pieces.reshape(NV * few, 128).T[:rows, :]

    @pl.when(is_root)
    def _():
        for d in range(NV):
            arrived(sample_in.at[(v + NV - d) % NV], sample_recv.at[d])
            arrived(solved_in.at[(v + NV - d) % NV], solved_recv.at[d])
        sample_ref[...] = sample_in[...].reshape(NV * few, 128).T[:rows, :]
        answer_ref[...] = solved_in[...].reshape(NV * few, 128).T[:rows, :]

    for d in range(1, NV):
        rhs_copy(d).wait_send()

    def gx_sent(g):
        for i in range(2 * NX - 1):
            gx_copy(g, i).wait_send()

    @pl.when(is_root)
    def _():
        move_inv().wait_send()
        move_rhs().wait_send()

    @pl.when(not_root)
    def _():
        gx_sent(0)
        for k in range(slots):

            @pl.when(level + k < slots)
            def _():
                gx_sent(k + 1)

        def gy_sent(yy):
            for d in ORDER:
                for j in range(NX):
                    gy_copy(yy, d, j).wait_send()
                gs_copy(yy, d).wait_send()

        each_y(gy_sent)
        for d in range(1, NV):
            sample_copy(d).wait_send()

    @pl.when(has_kids)
    def _():
        for d in range(1, NV):
            solved_copy(d).wait_send()
        for d in ORDER:
            own_copy(d).wait_send()
        for d in range(1, NY):
            row_copy(d).wait_send()
        for i, child in enumerate((left, right)):
            for w in range(NY):
                down0_copy(w, child, i).wait_send()
            for k in range(slots - 1):

                @pl.when(level + k < slots)
                def _():
                    down_copy(k, child, i).wait_send()

    @pl.when(has_parent)
    def _():
        @pl.when(inner == 1)
        def _():
            for w in range(NY):
                up0_copy(w).wait_send()

        for k in range(1, slots):

            @pl.when(level + k < slots)
            def _():
                up_copy(k).wait_send()

    def share_sent():
        for d in ORDER:
            share_copy(d).wait_send()

    @pl.when(is_leaf)
    def _():
        share_sent()
        leaf_copy().wait_send()
        for d in range(1, NY * NV):
            last_copy(d).wait_send()

    @pl.when(level == 1)
    def _():
        share_sent()

    @pl.when(is_top)
    def _():
        share_sent()
        gx_sent(last)
        for d in range(NV):
            top_copy(0, d).wait_send()
            top_copy(1, d).wait_send()


def on_device(nodes, rhs, panel, inverse_t, pattern):
    rows, count = rhs.shape[1:]
    slots = panel.shape[1]
    width = inverse_t.shape[2]
    span = NV * rows
    few = count // NV
    f32, bf16 = jnp.float32, jnp.bfloat16
    dma = pltpu.SemaphoreType.DMA
    vmem = pl.BlockSpec(memory_space=pltpu.VMEM)
    outs = pl.pallas_call(
        functools.partial(kernel, nodes),
        out_shape=[jax.ShapeDtypeStruct((rows, count), f32)] * 2,
        in_specs=[pl.BlockSpec(memory_space=pltpu.HBM)] * 4,
        out_specs=[vmem, vmem],
        scratch_shapes=[
            pltpu.VMEM((rows, count), f32),
            pltpu.VMEM((slots, rows, width), bf16),
            pltpu.SMEM(pattern.shape[1:], jnp.int32),
            pltpu.VMEM((slots, NX, 2, rows, width), bf16),
            pltpu.VMEM((NY, NX, 2, rows, width), bf16),
            pltpu.VMEM((NX, 2, rows, width), bf16),
            pltpu.VMEM((NV, few, 128), f32),
            pltpu.VMEM((NV, few, 128), f32),
            pltpu.VMEM((few, width), f32),
            pltpu.VMEM((few, span), f32),
            pltpu.VMEM((2, few, width), bf16),
            pltpu.VMEM((2**slots - 1, few, span), bf16),
            pltpu.VMEM((slots, few, span), bf16),
            pltpu.VMEM((NY, few, width), bf16),
            pltpu.VMEM((few, width), f32),
            pltpu.VMEM((few, width), f32),
            pltpu.VMEM((NV, few, 128), f32),
            pltpu.VMEM((NV, few, 128), f32),
            pltpu.VMEM((NY, few, span), bf16),
            pltpu.VMEM((slots, few, span), bf16),
            pltpu.VMEM((NY, few, span), bf16),
            pltpu.VMEM((NY, few, span), bf16),
            pltpu.VMEM((NV, few, 128), f32),
            pltpu.VMEM((NV, few, 128), f32),
            pltpu.VMEM((2, NV, few, 128), f32),
            pltpu.VMEM((few, width), f32),
            pltpu.VMEM((few, span), f32),
        ]
        + [dma((slots + 2, 2 * NX - 1))] * 2
        + [dma((NY, NX))] * 2
        + [dma((NY,))] * 2
        + [dma((NV,))] * 2
        + [dma((NY,))] * 2
        + [dma((NY,))] * 2
        + [dma((NY,)), dma((2, NY))]
        + [dma((slots,)), dma((2**slots - 1,))]
        + [dma((2, NY)), dma((NY,))]
        + [dma((2, slots)), dma((slots,))]
        + [dma((NY,))] * 2
        + [dma((NV,))] * 4
        + [dma((2,))] * 2
        + [dma((2, NV))]
        + [dma((4,)), pltpu.VMEM((2, span, width), bf16)]
        + [pltpu.VMEM((NY, NV, few, 128), bf16), pltpu.VMEM((NY * NV, few, 128), bf16)]
        + [dma((NY * NV,))] * 2,
        compiler_params=pltpu.CompilerParams(
            collective_id=0, has_side_effects=True, vmem_limit_bytes=56 * 2**20
        ),
    )(rhs[0], panel[0], inverse_t[0], pattern[0])
    return outs[0][None], outs[1][None]


def solution(mesh):
    in_specs = (
        P("lvl", "col", None),
        P("lvl", None, "col", None),
        P("lvl", "col", None),
        P("lvl", None, None, None),
    )
    out_specs = (P("lvl", "col", None), P("lvl", "col", None))
    return jax.shard_map(
        functools.partial(on_device, mesh.shape["lvl"]),
        mesh=mesh,
        in_specs=in_specs,
        out_specs=out_specs,
        check_vma=False,
    )
```

```python
import functools

import jax
import jax.numpy as jnp
from jax import lax
from jax.experimental import pallas as pl
from jax.experimental.pallas import tpu as pltpu
from jax.sharding import PartitionSpec as P

MESH = pl.DeviceIdType.MESH
NT = (((1,), (1,)), ((), ()))
NX = 4
NY = 4
NV = 2 * NX
ORDER = (1, 3, 2)


def remote(src, dst, send_sem, recv_sem, lvl, col):
    return pltpu.make_async_remote_copy(
        src_ref=src,
        dst_ref=dst,
        send_sem=send_sem,
        recv_sem=recv_sem,
        device_id=(lvl, col),
        device_id_type=MESH,
    )


def arrived(dst, sem):
    pltpu.make_async_copy(dst, dst, sem).wait()


def kernel(
    nodes,
    rhs_ref,
    panel_ref,
    inverse_ref,
    pattern_ref,
    sample_ref,
    answer_ref,
    rhs_own,
    panel_own,
    pattern_own,
    factor,
    inv,
    top_inv,
    turned,
    rhs_in,
    rhs_all,
    top_rhs,
    first_in,
    later_in,
    push,
    shares,
    sample_t,
    total,
    piece_out,
    sample_in,
    parent_in,
    above,
    part_out,
    own_in,
    solved_out,
    solved_in,
    top_piece,
    root_sample,
    root_solved,
    gx_send,
    gx_recv,
    gy_send,
    gy_recv,
    gs_send,
    gs_recv,
    rhs_send,
    rhs_recv,
    row_send,
    row_recv,
    share_send,
    share_recv,
    up0_send,
    up0_recv,
    up_send,
    up_recv,
    down0_send,
    down0_recv,
    down_send,
    down_recv,
    own_send,
    own_recv,
    sample_send,
    sample_recv,
    solved_send,
    solved_recv,
    move_send,
    move_recv,
    top_send,
    load_sem,
    joint,
    last_out,
    last_in,
    last_send,
    last_recv,
):
    rows = rhs_ref.shape[0]
    width = inv.shape[-1]
    slots = panel_ref.shape[0]
    tiles = pattern_ref.shape[2]
    tile = width // tiles
    span = NV * rows
    few = rhs_ref.shape[1] // NV
    f32, bf16 = jnp.float32, jnp.bfloat16
    root, top = nodes - 1, nodes // 2 - 1

    s = lax.axis_index("lvl")
    c = lax.axis_index("col")
    y, v = c // NV, c % NV
    x, core = v // 2, v % 2
    other = 1 - core

    level = 0
    step = 1
    for e in range(1, slots + 1):
        whole = 1 - ((s + 1) % 2**e + 2**e - 1) // 2**e
        level = level + whole
        step = step + whole * 2 ** (e - 1)
    side = (s // (2 * step)) % 2
    parent = (s + step * (1 - 2 * side)) % nodes
    above_at = [parent]
    for k in range(1, slots):
        far = step * 2**k
        above_at.append(
            (above_at[-1] + far * (1 - 2 * ((above_at[-1] // (2 * far)) % 2)) + nodes) % nodes
        )
    left = (s + nodes - step // 2) % nodes
    right = (s + step // 2) % nodes
    one_root = (s + 1) // nodes
    one_top = (level + 1) // slots - one_root
    inner = s % 2
    is_root = one_root == 1
    is_top = one_top == 1
    not_root = one_root == 0
    is_leaf = inner == 0
    has_kids = inner * (1 - one_root) == 1
    has_parent = one_root + one_top == 0

    def chip(yy, xx, cc):
        return (yy * NX + xx) * 2 + cc

    own_span = pl.ds(pl.multiple_of(y * span, 128), span)

    barrier = pltpu.get_barrier_semaphore()

    def greet(lvl, col):
        pl.semaphore_signal(barrier, inc=1, device_id=(lvl, col), device_id_type=MESH)

    @pl.when(is_leaf)
    def _():
        for d in range(1, NY * NV):
            greet(s, (c + d) % (NY * NV))

    @pl.when(inner == 1)
    def _():
        for d in range(1, NV):
            greet(s, y * NV + (v + d) % NV)
        for d in range(1, NY):
            greet(s, (y + d) % NY * NV + v)

    @pl.when(has_parent)
    def _():
        for w in range(NY):
            greet(parent, w * NV + v)

    @pl.when(has_kids)
    def _():
        for w in range(NY):
            greet(left, w * NV + v)
            greet(right, w * NV + v)

    @pl.when(is_top)
    def _():
        for q in range(NV):
            greet(root, y * NV + q)

    @pl.when(is_root)
    def _():
        for q in range(NV):
            greet(top, y * NV + q)

    def below(t):
        return [i for i in range(2 ** (t + 1) - 1) if i != 2**t - 1]

    for t in range(2, slots):

        @pl.when(level == t)
        def _(t=t):
            for i in below(t):
                if (i + 1) % 2 ** (t - 1):
                    greet((s + nodes - 2**t + 1 + i) % nodes, c)

    far_count = 0
    for k in range(2, slots):
        far_count = far_count + (slots - 1 - level + slots - k) // slots

    loads = (
        pltpu.make_async_copy(rhs_ref, rhs_own, load_sem.at[0]),
        pltpu.make_async_copy(inverse_ref, inv.at[y, x, core], load_sem.at[1]),
        pltpu.make_async_copy(pattern_ref, pattern_own, load_sem.at[2]),
        pltpu.make_async_copy(panel_ref, panel_own, load_sem.at[3]),
    )
    for load in loads:
        load.start()
    piece = 16

    def mask_slot(k):
        for q in range(rows // piece):
            tile_row = (c * rows + q * piece) // tile
            for j in range(tiles):
                keep = pattern_own[k, tile_row, j].astype(f32)
                part = (slice(q * piece, (q + 1) * piece), slice(j * tile, (j + 1) * tile))
                block = panel_own[(k,) + part]
                factor[(k, x, core) + part] = (block.astype(f32) * keep).astype(bf16)

    loads[0].wait()
    padded = jnp.concatenate(
        [rhs_own[...], jnp.zeros((128 - rows, rhs_ref.shape[1]), f32)], axis=0
    )
    turned[...] = padded.T.reshape(NV, few, 128)
    rhs_in[v] = turned[v]
    loads[1].wait()

    pl.semaphore_wait(
        barrier,
        (NV - 1 + NY - 1) * inner
        + (NV * NY - 1) * (1 - inner)
        + NY * (1 - one_root - one_top)
        + 2 * NY * inner * (1 - one_root)
        + NV * (one_top + one_root)
        + far_count,
    )

    last = slots + 1

    def block(g, xx, cc):
        if g == 0:
            return inv.at[y, xx, cc]
        if g == last:
            return top_inv.at[xx, cc]
        return factor.at[g - 1, xx, cc]

    def gx_copy(g, i):
        if i == 0:
            ref, col = block(g, x, core), chip(y, x, other)
        elif i < NX:
            ref, col = block(g, x, core), chip(y, (x + i) % NX, core)
        else:
            ref, col = block(g, (x + 2 * NX - 1 - i) % NX, core), chip(y, x, other)
        return remote(ref, ref, gx_send.at[g, i], gx_recv.at[g, i], s, col)

    def gx_wait(g, i):
        if i == 0:
            ref = block(g, x, other)
        elif i < NX:
            ref = block(g, (x + NX - i) % NX, core)
        else:
            ref = block(g, (x + 2 * NX - 1 - i) % NX, other)
        arrived(ref, gx_recv.at[g, i])

    def gx_start(g):
        for i in ORDER + (0,):
            gx_copy(g, i).start()

    def gx_pass(g, then=None):
        for i in ORDER:
            gx_wait(g, i)
            gx_copy(g, i + NX - 1).start()
            if then is not None:
                then(NX - i)

    def gx_finish(g):
        for i in (0,) + tuple(i + NX - 1 for i in ORDER):
            gx_wait(g, i)

    def each_y(body):
        for yy in range(NY):

            @pl.when(y == yy)
            def _(yy=yy):
                body(yy)

    def gy_copy(yy, d, j):
        ref = inv.at[yy, (x + j) % NX, core, :, yy * span :]
        col = chip((yy + d) % NY, x, core)
        return remote(ref, ref, gy_send.at[d, j], gy_recv.at[d, j], s, col)

    def gs_copy(yy, d):
        source = (yy + NY - d) % NY
        ref = inv.at[source, :, core, :, source * span :]
        return remote(ref, ref, gs_send.at[d], gs_recv.at[d], s, chip(yy, x, other))

    def gy_start(j):
        def body(yy):
            for d in ORDER:
                gy_copy(yy, d, j).start()

        each_y(body)

    def gy_pass():
        def body(yy):
            for d in ORDER:
                source = (yy + NY - d) % NY
                for j in range(NX):
                    arrived(
                        inv.at[source, (x + j) % NX, core, :, source * span :], gy_recv.at[d, j]
                    )
                gs_copy(yy, d).start()

        each_y(body)

    def gy_finish():
        def body(yy):
            for d in ORDER:
                source = (yy + NY - d) % NY
                arrived(inv.at[source, :, other, :, source * span :], gs_recv.at[d])

        each_y(body)

    def rhs_copy(d):
        to = (v + d) % NV
        return remote(turned.at[to], rhs_in.at[v], rhs_send.at[d], rhs_recv.at[d], s, y * NV + to)

    def row_copy(d):
        ref = rhs_all.at[:, own_span]
        return remote(ref, ref, row_send.at[d], row_recv.at[d], s, (y + d) % NY * NV + v)

    def rows_arrived():
        for d in range(1, NY):
            group_of = (y + NY - d) % NY
            arrived(
                rhs_all.at[:, pl.ds(pl.multiple_of(group_of * span, 128), span)], row_recv.at[d]
            )

    lane = lax.broadcasted_iota(jnp.int32, (few, 128), 1)

    def join_rhs():
        for d in range(1, NV):
            arrived(rhs_in.at[(v + NV - d) % NV], rhs_recv.at[d])
        joined = [jnp.zeros((few, 128), f32) for _ in range(span // 128)]
        for q in range(NV):
            a, b = divmod(q * rows, 128)
            moved = pltpu.roll(rhs_in[q], b, axis=1) if b else rhs_in[q]
            if b + rows <= 128:
                joined[a] = joined[a] + moved
            else:
                joined[a] = joined[a] + jnp.where(lane >= b, moved, 0.0)
                joined[a + 1] = joined[a + 1] + jnp.where(lane >= b, 0.0, moved)
        rhs_all[:, own_span] = jnp.concatenate(joined, axis=1)

    def share_copy(d):
        ref = shares.at[y]
        return remote(ref, ref, share_send.at[d], share_recv.at[d], s, (y + d) % NY * NV + v)

    def share_start(residual, rows_of):
        product = jnp.dot(residual, rows_of.reshape(span, width), preferred_element_type=f32)
        shares[y] = product.astype(bf16)
        for d in ORDER:
            share_copy(d).start()

    def share_sum():
        for d in ORDER:
            arrived(shares.at[(y + NY - d) % NY], share_recv.at[d])
        summed = shares[0].astype(f32)
        for w in range(1, NY):
            summed = summed + shares[w].astype(f32)
        return summed

    def up0_copy(w):
        return remote(
            push.at[0],
            first_in.at[side, :, own_span],
            up0_send.at[w],
            up0_recv.at[side, y],
            parent,
            w * NV + v,
        )

    def leaf_copy():
        return remote(
            push.at[0],
            first_in.at[side, :, own_span],
            up0_send.at[0],
            up0_recv.at[side, y],
            parent,
            c,
        )

    def up_copy(k):
        return remote(
            push.at[k],
            later_in.at[s % (step * 2 ** (k + 1))],
            up_send.at[k],
            up_recv.at[s % (step * 2 ** (k + 1))],
            above_at[k - 1],
            y * NV + v,
        )

    def flat(k):
        return factor[k].reshape(span, width)

    def pushed(k, sample_half):
        return lax.dot_general(sample_half, flat(k), NT, preferred_element_type=f32)

    def cut_pieces(ref, value):
        parts = [value[:, 128 * a : 128 * (a + 1)] for a in range(span // 128)]
        for q in range(NV):
            a, b = divmod(q * rows, 128)
            moved = pltpu.roll(parts[a], 128 - b, axis=1) if b else parts[a]
            if b + rows > 128:
                after = pltpu.roll(parts[a + 1], 128 - b, axis=1)
                moved = jnp.where(lane < 128 - b, moved, after)
            ref[q] = moved.astype(ref.dtype)

    def sample_copy(d):
        to = (v + d) % NV
        return remote(
            piece_out.at[to], sample_in.at[v], sample_send.at[d], sample_recv.at[d], s, y * NV + to
        )

    def solved_copy(d):
        to = (v + d) % NV
        return remote(
            solved_out.at[to], solved_in.at[v], solved_send.at[d], solved_recv.at[d], s, y * NV + to
        )

    def last_copy(d):
        to = (c + d) % (NY * NV)
        return remote(
            last_out.at[to // NV, to % NV],
            last_in.at[c],
            last_send.at[d],
            last_recv.at[d],
            s,
            to,
        )

    def top_copy(i, d):
        to = (v + d) % NV
        ref, sem = (sample_in, sample_recv) if i == 0 else (solved_in, solved_recv)
        return remote(
            top_piece.at[i, to], ref.at[v], top_send.at[i, d], sem.at[d], root, y * NV + to
        )

    def sample_out():
        cut_pieces(piece_out, sample_t[:, own_span])
        sample_in[v] = piece_out[v]
        for d in range(1, NV):
            sample_copy(d).start()

    def move_inv():
        return remote(
            inv.at[y, x, core], top_inv.at[x, core], move_send.at[0], move_recv.at[0], top, c
        )

    def move_rhs():
        return remote(
            rhs_all.at[:, own_span], top_rhs, move_send.at[1], move_recv.at[1], top, c
        )

    def down_copy(k, child, i):
        return remote(
            above.at[k],
            above.at[k + 1],
            down_send.at[i, k],
            down_recv.at[k + 1],
            child,
            y * NV + v,
        )

    def down0_copy(w, child, i):
        return remote(
            part_out.at[w],
            parent_in.at[y],
            down0_send.at[i, w],
            down0_recv.at[y],
            child,
            w * NV + v,
        )

    def own_copy(d):
        to = (y + d) % NY
        return remote(part_out.at[to], own_in.at[y], own_send.at[d], own_recv.at[d], s, to * NV + v)

    def hand_down(k):
        @pl.when(has_kids)
        def _():
            down_copy(k, left, 0).start()
            down_copy(k, right, 1).start()

    def make_joint(k):
        def some_rows(r, carry):
            at = pl.ds(pl.multiple_of(r * 2 * rows, 2 * rows), 2 * rows)
            for w in range(NY):
                start = w * span
                joint[k, at, start : start + span] = lax.dot_general(
                    factor[k, r, :, :, start:].reshape(2 * rows, width - start),
                    inv[w, :, :, :, start:].reshape(span, width - start),
                    NT,
                    preferred_element_type=f32,
                ).astype(bf16)
            return carry

        lax.fori_loop(0, NX, some_rows, 0)

    def make_base():
        group = lax.broadcasted_iota(jnp.int32, (few, width), 1) // span
        total[...] = jnp.where(group == y, sample_t[...], 0.0)
        for k in range(slots - 1, 1, -1):

            @pl.when(level + k < slots)
            def _():
                arrived(above.at[k], down_recv.at[k])
                if k < slots - 1:
                    hand_down(k)
                total[...] -= jnp.dot(above[k], flat(k), preferred_element_type=f32)

        back = total[...].astype(bf16)
        for w in range(NY):
            start = w * span
            total[:, start : start + span] = lax.dot_general(
                back[:, start:],
                inv[w, :, :, :, start:].reshape(span, width - start),
                NT,
                preferred_element_type=f32,
            )

    @pl.when(is_leaf)
    def _():
        gx_start(0)
        for d in range(1, NV):
            rhs_copy(d).start()
        loads[2].wait()
        loads[3].wait()
        for k in range(slots):
            mask_slot(k)
            if k == 0:
                gx_start(1)
        gx_pass(0)
        join_rhs()
        gx_finish(0)
        share_start(rhs_all[:, own_span].astype(bf16), inv[y])
        if slots > 1:
            gx_start(2)
        gx_pass(1, lambda j: gx_start(3) if j == 3 and slots > 2 else None)
        sample_t[...] = share_sum()
        sample_half = sample_t[...].astype(bf16)
        for k in range(slots):
            if k > 0:
                gx_pass(
                    k + 1, lambda j: gx_start(k + 3) if j == 3 and k + 3 <= slots else None
                )
            gx_finish(k + 1)
            push[k] = pushed(k, sample_half).astype(bf16)
            if k == 0:
                leaf_copy().start()
                for j in range(NX):
                    gy_start(j)
            else:
                up_copy(k).start()

    @pl.when(inner == 1)
    def _():
        @pl.when(is_root)
        def _():
            move_inv().start()

        @pl.when(not_root)
        def _():
            gx_start(0)
            gy_start(0)

        for d in range(1, NV):
            rhs_copy(d).start()
        loads[2].wait()
        loads[3].wait()
        for k in range(max(slots - 1, 1)):
            mask_slot(k)

        @pl.when(not_root)
        def _():
            def follow(j):
                gy_start(j)
                if j == 3:
                    gx_start(1)

            gx_pass(0, follow)

        join_rhs()

        @pl.when(is_root)
        def _():
            move_rhs().start()

        @pl.when(not_root)
        def _():
            for d in range(1, NY):
                row_copy(d).start()
            gx_pass(1)
            for k in range(1, slots - 1):

                @pl.when(level + k < slots)
                def _():
                    gx_start(k + 1)

            @pl.when(is_top)
            def _():
                arrived(top_inv.at[x, core], move_recv.at[0])
                gx_start(last)

            @pl.when(level == 1)
            def _():
                gx_finish(0)
                for i in range(2):
                    arrived(first_in.at[i, :, own_span], up0_recv.at[i, y])
                incoming = first_in[0, :, own_span].astype(f32) + first_in[
                    1, :, own_span
                ].astype(f32)
                share_start((rhs_all[:, own_span] - incoming).astype(bf16), inv[y])
                gx_finish(1)
                sample_t[...] = share_sum()

            @pl.when(level > 1)
            def _():
                gy_pass()
                rows_arrived()
                gy_finish()
                gx_finish(0)
                gx_finish(1)

                @pl.when(is_top)
                def _():
                    gx_pass(last)
                    gx_finish(last)
                    arrived(top_rhs, move_recv.at[1])
                    make_joint(0)

                for i in range(2):
                    for w in range(NY):
                        arrived(first_in.at[i, :, w * span : (w + 1) * span], up0_recv.at[i, w])
                incoming = first_in[0].astype(f32) + first_in[1].astype(f32)
                residual = (rhs_all[...] - incoming).astype(bf16)
                for w in range(NY):
                    to = (w + 1) * span
                    sample_t[:, w * span : to] = jnp.dot(
                        residual[:, :to],
                        inv[: w + 1, :, :, :, w * span : to].reshape(to, span),
                        preferred_element_type=f32,
                    )

            sample_half = sample_t[...].astype(bf16)

            def pushed_sum(t):
                out = pushed(0, sample_half)
                for i in below(t):
                    arrived(later_in.at[i], up_recv.at[i])
                    out = out + later_in[i].astype(f32)
                return out

            for t in range(1, slots - 1):

                @pl.when(level == t)
                def _(t=t):
                    push[0] = pushed_sum(t).astype(bf16)
                    for w in range(NY):
                        up0_copy(w).start()

            @pl.when(is_top)
            def _():
                residual_root = (top_rhs[...] - pushed_sum(slots - 1)).astype(bf16)
                share_start(residual_root, top_inv[...])
                make_base()
                root_t = share_sum()
                root_sample[...] = root_t
                solved_root = lax.dot_general(
                    root_t.astype(bf16),
                    top_inv[...].reshape(span, width),
                    NT,
                    preferred_element_type=f32,
                )
                root_solved[...] = solved_root
                above[0] = solved_root.astype(bf16)
                down_copy(0, left, 0).start()
                down_copy(0, right, 1).start()

            for k in range(1, slots - 1):

                @pl.when(level + k < slots)
                def _():
                    gx_pass(k + 1)
                    gx_finish(k + 1)
                    push[k] = pushed(k, sample_half).astype(bf16)
                    up_copy(k).start()

    @pl.when(has_parent)
    def _():
        sample_out()

        @pl.when(level < 2)
        def _():
            gy_pass()

            @pl.when(level == 1)
            def _():
                rows_arrived()

            gy_finish()

        def one_joint(k, carry):
            make_joint(k)
            return carry

        lax.fori_loop(0, min(slots, 2), one_joint, 0)

    @pl.when(not_root)
    def _():
        @pl.when(has_parent)
        def _():
            make_base()

            @pl.when(level + 1 < slots)
            def _():
                arrived(above.at[1], down_recv.at[1])
                hand_down(1)
                total[...] -= jnp.dot(above[1], joint[1], preferred_element_type=f32)

            for w in range(NY):
                arrived(parent_in.at[w], down0_recv.at[w])
            summed = parent_in[0].astype(f32)
            for w in range(1, NY):
                summed = summed + parent_in[w].astype(f32)
            above[0] = summed.astype(bf16)
            hand_down(0)

        for w in range(NY):
            lanes = slice(w * span, (w + 1) * span)
            part = total[:, lanes] - jnp.dot(
                above[0], joint[0, :, lanes], preferred_element_type=f32
            )
            part_out[w] = part.astype(bf16)

            @pl.when(is_leaf)
            def _():
                cut_pieces(last_out.at[w], part)

            @pl.when(has_kids)
            def _():
                down0_copy(w, left, 0).start()
                down0_copy(w, right, 1).start()

        @pl.when(is_leaf)
        def _():
            last_in[c] = last_out[y, v]
            for d in range(1, NY * NV):
                last_copy(d).start()

        @pl.when(has_kids)
        def _():
            own_in[y] = part_out[y]
            for d in ORDER:
                own_copy(d).start()

        @pl.when(is_top)
        def _():
            cut_pieces(top_piece.at[0], root_sample[:, own_span])
            cut_pieces(top_piece.at[1], root_solved[...])
            for d in range(NV):
                top_copy(0, d).start()
                top_copy(1, d).start()
            sample_out()

        for d in range(1, NV):
            arrived(sample_in.at[(v + NV - d) % NV], sample_recv.at[d])
        sample_ref[...] = sample_in[...].reshape(NV * few, 128).T[:rows, :]

        @pl.when(has_kids)
        def _():
            for d in ORDER:
                arrived(own_in.at[(y + NY - d) % NY], own_recv.at[d])
            solved = own_in[0].astype(f32)
            for w in range(1, NY):
                solved = solved + own_in[w].astype(f32)
            cut_pieces(solved_out, solved)
            solved_in[v] = solved_out[v]
            for d in range(1, NV):
                solved_copy(d).start()
            for d in range(1, NV):
                arrived(solved_in.at[(v + NV - d) % NV], solved_recv.at[d])
            answer_ref[...] = solved_in[...].reshape(NV * few, 128).T[:rows, :]

        @pl.when(is_leaf)
        def _():
            for d in range(1, NY * NV):
                source = (c + NY * NV - d) % (NY * NV)
                arrived(last_in.at[source], last_recv.at[d])
            pieces = last_in[0:NV].astype(f32)
            for w in range(1, NY):
                pieces = pieces + last_in[w * NV : (w + 1) * NV].astype(f32)
            answer_ref[...] = pieces.reshape(NV * few, 128).T[:rows, :]

    @pl.when(is_root)
    def _():
        for d in range(NV):
            arrived(sample_in.at[(v + NV - d) % NV], sample_recv.at[d])
            arrived(solved_in.at[(v + NV - d) % NV], solved_recv.at[d])
        sample_ref[...] = sample_in[...].reshape(NV * few, 128).T[:rows, :]
        answer_ref[...] = solved_in[...].reshape(NV * few, 128).T[:rows, :]

    for d in range(1, NV):
        rhs_copy(d).wait_send()

    def gx_sent(g):
        for i in range(2 * NX - 1):
            gx_copy(g, i).wait_send()

    @pl.when(is_root)
    def _():
        move_inv().wait_send()
        move_rhs().wait_send()

    @pl.when(not_root)
    def _():
        gx_sent(0)
        for k in range(slots):

            @pl.when(level + k < slots)
            def _():
                gx_sent(k + 1)

        def gy_sent(yy):
            for d in ORDER:
                for j in range(NX):
                    gy_copy(yy, d, j).wait_send()
                gs_copy(yy, d).wait_send()

        each_y(gy_sent)
        for d in range(1, NV):
            sample_copy(d).wait_send()

    @pl.when(has_kids)
    def _():
        for d in range(1, NV):
            solved_copy(d).wait_send()
        for d in ORDER:
            own_copy(d).wait_send()
        for d in range(1, NY):
            row_copy(d).wait_send()
        for i, child in enumerate((left, right)):
            for w in range(NY):
                down0_copy(w, child, i).wait_send()
            for k in range(slots - 1):

                @pl.when(level + k < slots)
                def _():
                    down_copy(k, child, i).wait_send()

    @pl.when(has_parent)
    def _():
        @pl.when(inner == 1)
        def _():
            for w in range(NY):
                up0_copy(w).wait_send()

        for k in range(1, slots):

            @pl.when(level + k < slots)
            def _():
                up_copy(k).wait_send()

    def share_sent():
        for d in ORDER:
            share_copy(d).wait_send()

    @pl.when(is_leaf)
    def _():
        share_sent()
        leaf_copy().wait_send()
        for d in range(1, NY * NV):
            last_copy(d).wait_send()

    @pl.when(level == 1)
    def _():
        share_sent()

    @pl.when(is_top)
    def _():
        share_sent()
        gx_sent(last)
        for d in range(NV):
            top_copy(0, d).wait_send()
            top_copy(1, d).wait_send()


def on_device(nodes, rhs, panel, inverse_t, pattern):
    rows, count = rhs.shape[1:]
    slots = panel.shape[1]
    width = inverse_t.shape[2]
    span = NV * rows
    few = count // NV
    f32, bf16 = jnp.float32, jnp.bfloat16
    dma = pltpu.SemaphoreType.DMA
    vmem = pl.BlockSpec(memory_space=pltpu.VMEM)
    outs = pl.pallas_call(
        functools.partial(kernel, nodes),
        out_shape=[jax.ShapeDtypeStruct((rows, count), f32)] * 2,
        in_specs=[pl.BlockSpec(memory_space=pltpu.HBM)] * 4,
        out_specs=[vmem, vmem],
        scratch_shapes=[
            pltpu.VMEM((rows, count), f32),
            pltpu.VMEM((slots, rows, width), bf16),
            pltpu.SMEM(pattern.shape[1:], jnp.int32),
            pltpu.VMEM((slots, NX, 2, rows, width), bf16),
            pltpu.VMEM((NY, NX, 2, rows, width), bf16),
            pltpu.VMEM((NX, 2, rows, width), bf16),
            pltpu.VMEM((NV, few, 128), f32),
            pltpu.VMEM((NV, few, 128), f32),
            pltpu.VMEM((few, width), f32),
            pltpu.VMEM((few, span), f32),
            pltpu.VMEM((2, few, width), bf16),
            pltpu.VMEM((2**slots - 1, few, span), bf16),
            pltpu.VMEM((slots, few, span), bf16),
            pltpu.VMEM((NY, few, width), bf16),
            pltpu.VMEM((few, width), f32),
            pltpu.VMEM((few, width), f32),
            pltpu.VMEM((NV, few, 128), f32),
            pltpu.VMEM((NV, few, 128), f32),
            pltpu.VMEM((NY, few, span), bf16),
            pltpu.VMEM((slots, few, span), bf16),
            pltpu.VMEM((NY, few, span), bf16),
            pltpu.VMEM((NY, few, span), bf16),
            pltpu.VMEM((NV, few, 128), f32),
            pltpu.VMEM((NV, few, 128), f32),
            pltpu.VMEM((2, NV, few, 128), f32),
            pltpu.VMEM((few, width), f32),
            pltpu.VMEM((few, span), f32),
        ]
        + [dma((slots + 2, 2 * NX - 1))] * 2
        + [dma((NY, NX))] * 2
        + [dma((NY,))] * 2
        + [dma((NV,))] * 2
        + [dma((NY,))] * 2
        + [dma((NY,))] * 2
        + [dma((NY,)), dma((2, NY))]
        + [dma((slots,)), dma((2**slots - 1,))]
        + [dma((2, NY)), dma((NY,))]
        + [dma((2, slots)), dma((slots,))]
        + [dma((NY,))] * 2
        + [dma((NV,))] * 4
        + [dma((2,))] * 2
        + [dma((2, NV))]
        + [dma((4,)), pltpu.VMEM((2, span, width), bf16)]
        + [pltpu.VMEM((NY, NV, few, 128), bf16), pltpu.VMEM((NY * NV, few, 128), bf16)]
        + [dma((NY * NV,))] * 2,
        compiler_params=pltpu.CompilerParams(
            collective_id=0, has_side_effects=True, vmem_limit_bytes=56 * 2**20
        ),
    )(rhs[0], panel[0], inverse_t[0], pattern[0])
    return outs[0][None], outs[1][None]


def solution(mesh):
    in_specs = (
        P("lvl", "col", None),
        P("lvl", None, "col", None),
        P("lvl", "col", None),
        P("lvl", None, None, None),
    )
    out_specs = (P("lvl", "col", None), P("lvl", "col", None))
    return jax.shard_map(
        functools.partial(on_device, mesh.shape["lvl"]),
        mesh=mesh,
        in_specs=in_specs,
        out_specs=out_specs,
        check_vma=False,
    )
```
